256 devices in a mesh: comp: 2 (over y_hi), lat: 8 (over x, core), lon: 16 (over y_lo, z).
Axes of the slice: x: 4, y: 4 (y_hi: 2, y_lo: 2; y = y_hi * 2 + y_lo), z: 8, core: 2. Of those that a mesh axis runs over, the one named last changes fastest.
Arguments:
- atm_state: bfloat16 [32768, 512], P(('comp', 'lat', 'lon')), may hold values from -6 to 6
- edge_state: bfloat16 [32768, 6, 512], P(('comp', 'lat', 'lon')), may hold values from -6 to 6
- neighbours: int32 [32768, 6], P(('comp', 'lat', 'lon')), may hold values from 0 to 32767, as said below
- degree: int32 [32768], P(('comp', 'lat', 'lon')), may hold values from 5 to 6
- surface_fields: float32 [4, 512, 2048], P(None, ('comp', 'lat'), 'lon'), may hold values from -6 to 6
- ocean_state: bfloat16 [512, 2048, 256], P(('comp', 'lat'), 'lon'), may hold values from -6 to 6
- wet_mask: int32 [512, 2048], P(('comp', 'lat'), 'lon'), may hold values from 0 to 1, as said below
- flux_columns: int32 [4, 512, 2048], P(None, ('comp', 'lat'), 'lon'), may hold values from 0 to 32767, as said below
- flux_weights: float32 [4, 512, 2048], P(None, ('comp', 'lat'), 'lon'), may hold values from 0.1 to 1
- surface_columns: int32 [4, 32768], P(None, ('comp', 'lat', 'lon')), may hold values from 0 to 1048575, as said below
- surface_weights: float32 [4, 32768], P(None, ('comp', 'lat', 'lon')), may hold values from 0.1 to 1
- w_surface: float32 [4, 512], replicated, may hold values from -3 to 3
- w_flux: float32 [512, 4], replicated, may hold values from -0.25 to 0.25
- ln1_gain: float32 [512], replicated, may hold values from 0.5 to 1.5
- w_query: bfloat16 [512, 512], replicated, may hold values from -0.25 to 0.25
- w_key: bfloat16 [512, 512], replicated, may hold values from -0.25 to 0.25
- w_value: bfloat16 [512, 512], replicated, may hold values from -0.25 to 0.25
- w_out: bfloat16 [512, 512], replicated, may hold values from -0.25 to 0.25
- w_edge_in: bfloat16 [512, 512], replicated, may hold values from -0.25 to 0.25
- w_edge_src: bfloat16 [512, 512], replicated, may hold values from -0.25 to 0.25
- w_edge_dst: bfloat16 [512, 512], replicated, may hold values from -0.25 to 0.25
- w_edge_out: bfloat16 [512, 512], replicated, may hold values from -0.25 to 0.25
- w_bias: float32 [512, 8], replicated, may hold values from -0.25 to 0.25
- ln2_gain: float32 [512], replicated, may hold values from 0.5 to 1.5
- w_up: bfloat16 [512, 2048], replicated, may hold values from -0.25 to 0.25
- w_down: bfloat16 [2048, 512], replicated, may hold values from -0.125 to 0.125
- w_flux_in: float32 [4, 256], replicated, may hold values from -3 to 3
- dw_kernel: float32 [2, 49, 256], replicated, may hold values from -0.875 to 0.875
- dw_bias: float32 [2, 256], replicated, may hold values from -3 to 3
- ocean_gain: float32 [2, 256], replicated, may hold values from 0.5 to 1.5
- w_expand: bfloat16 [2, 256, 1024], replicated, may hold values from -0.375 to 0.375
- w_reduce: bfloat16 [2, 1024, 256], replicated, may hold values from -0.1875 to 0.1875
- layer_scale: float32 [2, 256], replicated, may hold values from 0.2 to 1
Outputs:
- atm_out: bfloat16 [32768, 512], P(('comp', 'lat', 'lon'))
- edge_out: bfloat16 [32768, 6, 512], P(('comp', 'lat', 'lon'))
- ocean_out: bfloat16 [512, 2048, 256], P(('comp', 'lat'), 'lon')
The draws below stay inside these ranges and needn't reach their ends.
Inputs may be any that keep to these rules, and one draw needn't show every extreme that they name: `neighbours`: slots beyond degree[n] hold n itself. A used slot names a node of the same partition, or one of the first 64 nodes of one of the eight partitions beside it (partitions are numbered row by row over 16 rows of 16, each holding 128 consecutive ids; columns wrap around, rows do not). `wet_mask`: the first and last 3 latitude rows are land. `flux_columns`: each ocean cell reads nodes of the partitions of its own row band (latitude row // 32), in any column. `surface_columns`: each node reads cells whose latitude row // 32 is its partition's row, in any longitude.
All inputs are finite; a program needn't handle non-finite values.
Results may differ from the reference program's by a relative error of at most 0.011.
Values may be sent and summed in bfloat16 or wider, within the bound.
A program may use at most 128 MiB of HBM per device.

```python
import math
import jax
import jax.numpy as jnp
from jax import lax

D = 512
HEADS = 8
FFN = 2048
DEG = 6
NODE_DEV = 128
BORDER = 64
NODES = 32768
C = 256
OHID = 1024
KS = 7
BLOCKS = 2
LAT_T = 32
LON_T = 128
NLAT = 512
NLON = 2048
FLUXC = 4
SURF = 4
NW = 4


def node_tables(key):
    key = jax.random.fold_in(key, 7101)
    subkeys = jax.random.split(key, 5)
    part_count = NODES // NODE_DEV
    lon_parts = NLON // LON_T
    row_parts = part_count // lon_parts
    node_ids = jnp.arange(NODES, dtype=jnp.int32)
    partition = node_ids // NODE_DEV
    row_inside = node_ids % NODE_DEV
    part_row = partition // lon_parts
    part_col = partition % lon_parts
    degree = DEG - 1 + jax.random.randint(subkeys[0], (NODES,), 0, 2)
    degree = jnp.where((row_inside == 0) | (row_inside == NODE_DEV - 1), DEG - 1, jnp.where(row_inside == 1, DEG, degree))
    remote = jax.random.randint(subkeys[1], (NODES, DEG), 0, 2)
    direction = jax.random.randint(subkeys[2], (NODES, DEG), 0, 8)
    direction = direction + (direction >= 4).astype(jnp.int32)
    step_row = direction // 3 - 1
    step_col = direction % 3 - 1
    target_row = part_row[:, None] + step_row
    step_row = jnp.where((target_row < 0) | (target_row >= row_parts), 0, step_row)
    target_part = (part_row[:, None] + step_row) * lon_parts + (part_col[:, None] + step_col) % lon_parts
    far_row = jax.random.randint(subkeys[3], (NODES, DEG), 0, BORDER)
    near_row = jax.random.randint(subkeys[4], (NODES, DEG), 0, NODE_DEV)
    target = jnp.where(remote == 1, target_part * NODE_DEV + far_row, partition[:, None] * NODE_DEV + near_row)
    slot_ids = jnp.arange(DEG)[None, :]
    target = jnp.where(slot_ids < degree[:, None], target, node_ids[:, None])
    return (target.astype(jnp.int32), degree.astype(jnp.int32))


def draw_neighbours(key, part):
    return node_tables(key)[0]


def draw_degree(key, part):
    return node_tables(key)[1]


def draw_wet_mask(key, part):
    key = jax.random.fold_in(key, 7202)
    subkeys = jax.random.split(key, 4)
    count = 24
    centre_lat = jax.random.randint(subkeys[0], (count,), 0, NLAT)
    centre_lon = jax.random.randint(subkeys[1], (count,), 0, NLON)
    half_lat = jax.random.randint(subkeys[2], (count,), 1, max(2, NLAT // 10))
    half_lon = jax.random.randint(subkeys[3], (count,), 1, max(2, NLON // 8))
    lat_ids = jnp.arange(NLAT)[:, None, None]
    lon_ids = jnp.arange(NLON)[None, :, None]
    lon_gap = jnp.abs((lon_ids - centre_lon + NLON // 2) % NLON - NLON // 2)
    inside = (jnp.abs(lat_ids - centre_lat) <= half_lat) & (lon_gap <= half_lon)
    rows_only = jnp.arange(NLAT)[:, None]
    polar = (rows_only < KS // 2) | (rows_only >= NLAT - KS // 2)
    land = jnp.any(inside, axis=2) | polar
    return jnp.where(land, 0, 1).astype(jnp.int32)


def draw_flux_columns(key, part):
    key = jax.random.fold_in(key, 7303)
    subkeys = jax.random.split(key, 2)
    lon_parts = NLON // LON_T
    band = jnp.arange(NLAT)[None, :, None] // LAT_T
    part_pick = jax.random.randint(subkeys[0], (NW, NLAT, NLON), 0, lon_parts)
    row_pick = jax.random.randint(subkeys[1], (NW, NLAT, NLON), 0, NODE_DEV)
    columns = (band * lon_parts + part_pick) * NODE_DEV + row_pick
    columns = columns.at[0, 0, 0].set(0).at[0, NLAT - 1, NLON - 1].set(NODES - 1)
    return columns.astype(jnp.int32)


def draw_surface_columns(key, part):
    key = jax.random.fold_in(key, 7404)
    subkeys = jax.random.split(key, 2)
    lon_parts = NLON // LON_T
    band = jnp.arange(NODES) // NODE_DEV // lon_parts
    lat_pick = band[None, :] * LAT_T + jax.random.randint(subkeys[0], (NW, NODES), 0, LAT_T)
    lon_pick = jax.random.randint(subkeys[1], (NW, NODES), 0, NLON)
    columns = lat_pick * NLON + lon_pick
    columns = columns.at[0, 0].set(0).at[0, NODES - 1].set(NLAT * NLON - 1)
    return columns.astype(jnp.int32)


def block_levels(rng, extent, shards, smallest, largest):
    factor_of, own = 1.0, jax.random.fold_in(rng, 6)
    for axis_at, parts in shards:
        steps = jnp.exp(jax.random.uniform(jax.random.fold_in(own, axis_at), (parts,), jnp.float32, smallest / len(shards), largest / len(shards)))
        factor_of = factor_of * jnp.repeat(steps, extent[axis_at] // parts).reshape([-1 if axis == axis_at else 1 for axis in range(len(extent))])
    return factor_of


def gaussian(key, extent, scale, most, cuts=(), kind=jnp.bfloat16):
    array = jax.random.normal(key, extent, jnp.float32) * scale
    if len(cuts) > 0:
        array = block_levels(key, extent, cuts, -0.22, 0.18) * array
    return jnp.clip(array, min=-most, max=most).astype(kind)


def setup_inputs(seed: int = 0) -> dict:
    arg_keys = jax.random.split(jax.random.key(seed), 34)
    atm_state = gaussian(arg_keys[0], (NODES, D), 1.0, 6.0, ((0, 256),))
    edge_state = gaussian(arg_keys[1], (NODES, DEG, D), 1.0, 6.0, ((0, 256),))
    neighbours = draw_neighbours(jax.random.fold_in(arg_keys[33], 71), 0)
    degree = draw_degree(jax.random.fold_in(arg_keys[33], 71), 0)
    surface_fields = gaussian(arg_keys[4], (SURF, NLAT, NLON), 1.0, 6.0, ((1, 16), (2, 16)), jnp.float32)
    ocean_state = gaussian(arg_keys[5], (NLAT, NLON, C), 1.0, 6.0, ((0, 16), (1, 16)))
    wet_mask = draw_wet_mask(jax.random.fold_in(arg_keys[33], 71), 0)
    flux_columns = draw_flux_columns(jax.random.fold_in(arg_keys[33], 71), 0)
    flux_weights = jnp.clip(0.1 + 0.9 * jax.random.uniform(arg_keys[8], (NW, NLAT, NLON), jnp.float32) ** block_levels(arg_keys[8], (NW, NLAT, NLON), ((1, 16), (2, 16)), -0.2, 0.2), 0.1, 1.0)
    surface_columns = draw_surface_columns(jax.random.fold_in(arg_keys[33], 71), 0)
    surface_weights = jnp.clip(0.1 + 0.9 * jax.random.uniform(arg_keys[10], (NW, NODES), jnp.float32) ** block_levels(arg_keys[10], (NW, NODES), ((1, 256),), -0.2, 0.2), 0.1, 1.0)
    w_surface = gaussian(arg_keys[11], (SURF, D), SURF ** -0.5, 3.0, (), jnp.float32)
    w_flux = gaussian(arg_keys[12], (D, FLUXC), D ** -0.5, 0.25, (), jnp.float32)
    ln1_gain = jnp.clip(1.0 + 0.1 * jax.random.normal(arg_keys[13], (D,), jnp.float32), 0.5, 1.5)
    w_query = gaussian(arg_keys[14], (D, D), D ** -0.5, 0.25)
    w_key = gaussian(arg_keys[15], (D, D), D ** -0.5, 0.25)
    w_value = gaussian(arg_keys[16], (D, D), D ** -0.5, 0.25)
    w_out = gaussian(arg_keys[17], (D, D), D ** -0.5, 0.25)
    w_edge_in = gaussian(arg_keys[18], (D, D), D ** -0.5, 0.25)
    w_edge_src = gaussian(arg_keys[19], (D, D), D ** -0.5, 0.25)
    w_edge_dst = gaussian(arg_keys[20], (D, D), D ** -0.5, 0.25)
    w_edge_out = gaussian(arg_keys[21], (D, D), D ** -0.5, 0.25)
    w_bias = gaussian(arg_keys[22], (D, HEADS), D ** -0.5, 0.25, (), jnp.float32)
    ln2_gain = jnp.clip(1.0 + 0.1 * jax.random.normal(arg_keys[23], (D,), jnp.float32), 0.5, 1.5)
    w_up = gaussian(arg_keys[24], (D, FFN), D ** -0.5, 0.25)
    w_down = gaussian(arg_keys[25], (FFN, D), FFN ** -0.5, 0.125)
    w_flux_in = gaussian(arg_keys[26], (FLUXC, C), FLUXC ** -0.5, 3.0, (), jnp.float32)
    dw_kernel = gaussian(arg_keys[27], (BLOCKS, KS * KS, C), (KS * KS) ** -0.5, 0.875, (), jnp.float32)
    dw_bias = gaussian(arg_keys[28], (BLOCKS, C), 0.5, 3.0, (), jnp.float32)
    ocean_gain = jnp.clip(1.0 + 0.1 * jax.random.normal(arg_keys[29], (BLOCKS, C), jnp.float32), 0.5, 1.5)
    w_expand = gaussian(arg_keys[30], (BLOCKS, C, OHID), C ** -0.5, 0.375)
    w_reduce = gaussian(arg_keys[31], (BLOCKS, OHID, C), OHID ** -0.5, 0.1875)
    layer_scale = jnp.clip(jnp.exp(jax.random.uniform(arg_keys[32], (BLOCKS, C), jnp.float32, math.log(0.2), math.log(1.0))), 0.2, 1.0)
    return dict(atm_state=atm_state, edge_state=edge_state, neighbours=neighbours, degree=degree, surface_fields=surface_fields, ocean_state=ocean_state, wet_mask=wet_mask, flux_columns=flux_columns, flux_weights=flux_weights, surface_columns=surface_columns, surface_weights=surface_weights, w_surface=w_surface, w_flux=w_flux, ln1_gain=ln1_gain, w_query=w_query, w_key=w_key, w_value=w_value, w_out=w_out, w_edge_in=w_edge_in, w_edge_src=w_edge_src, w_edge_dst=w_edge_dst, w_edge_out=w_edge_out, w_bias=w_bias, ln2_gain=ln2_gain, w_up=w_up, w_down=w_down, w_flux_in=w_flux_in, dw_kernel=dw_kernel, dw_bias=dw_bias, ocean_gain=ocean_gain, w_expand=w_expand, w_reduce=w_reduce, layer_scale=layer_scale)


def layer_norm(values, gain, epsilon):
    centre = values - lax.optimization_barrier(jnp.mean(values, axis=-1, keepdims=True))
    spread = lax.optimization_barrier(jnp.mean(centre * centre, axis=-1, keepdims=True))
    return centre * lax.rsqrt(spread + epsilon) * gain

def reference(atm_state, edge_state, neighbours, degree, surface_fields, ocean_state, wet_mask, flux_columns, flux_weights, surface_columns, surface_weights, w_surface, w_flux, ln1_gain, w_query, w_key, w_value, w_out, w_edge_in, w_edge_src, w_edge_dst, w_edge_out, w_bias, ln2_gain, w_up, w_down, w_flux_in, dw_kernel, dw_bias, ocean_gain, w_expand, w_reduce, layer_scale):
    highest = lax.Precision.HIGHEST
    head_dim = D // HEADS
    cells_flat = surface_fields.reshape(SURF, NLAT * NLON)
    picked = cells_flat[:, surface_columns]
    surface_nodes = lax.optimization_barrier(jnp.sum(picked * surface_weights[None], axis=1))
    atm_in = atm_state.astype(jnp.float32) + jnp.dot(surface_nodes.T, w_surface, precision=highest)
    normed = layer_norm(atm_in, ln1_gain, 1e-05).astype(jnp.bfloat16)
    queries = jnp.dot(normed, w_query, preferred_element_type=jnp.float32).astype(jnp.bfloat16)
    keys_all = jnp.dot(normed, w_key, preferred_element_type=jnp.float32).astype(jnp.bfloat16)
    values_all = jnp.dot(normed, w_value, preferred_element_type=jnp.float32).astype(jnp.bfloat16)
    far_part = jnp.dot(normed, w_edge_dst, preferred_element_type=jnp.float32).astype(jnp.bfloat16)
    own_part = jnp.dot(normed, w_edge_src, preferred_element_type=jnp.float32)
    flat_ids = neighbours.reshape(-1)
    edge_flat = edge_state.reshape(NODES * DEG, D)
    before = jnp.dot(edge_flat, w_edge_in, preferred_element_type=jnp.float32)
    before = before + jnp.repeat(own_part, DEG, axis=0) + far_part[flat_ids].astype(jnp.float32)
    edge_hidden = jax.nn.silu(before).astype(jnp.bfloat16)
    edge_sum = edge_flat.astype(jnp.float32) + jnp.dot(edge_hidden, w_edge_out, preferred_element_type=jnp.float32)
    edge_out = edge_sum.astype(jnp.bfloat16).reshape(NODES, DEG, D)
    bias = jnp.dot(edge_sum, w_bias, precision=highest).reshape(NODES, DEG, HEADS)
    query_heads = queries.astype(jnp.float32).reshape(NODES, HEADS, head_dim)
    key_rows = keys_all[neighbours].astype(jnp.float32).reshape(NODES, DEG, HEADS, head_dim)
    scores = jnp.einsum('nhd,nkhd->nkh', query_heads, key_rows, precision=highest) / math.sqrt(head_dim) + bias
    usable = jnp.arange(DEG)[None, :] < degree[:, None]
    scores = jnp.where(usable[:, :, None], scores, -1e+30)
    weights = jax.nn.softmax(scores, axis=1).astype(jnp.bfloat16)
    value_rows = values_all[neighbours].astype(jnp.float32).reshape(NODES, DEG, HEADS, head_dim)
    attended = jnp.einsum('nkh,nkhd->nhd', weights.astype(jnp.float32), value_rows, precision=highest)
    attended = attended.astype(jnp.bfloat16).reshape(NODES, D)
    atm_mid = atm_in + jnp.dot(attended, w_out, preferred_element_type=jnp.float32)
    normed2 = layer_norm(atm_mid, ln2_gain, 1e-05).astype(jnp.bfloat16)
    expanded = jax.nn.silu(jnp.dot(normed2, w_up, preferred_element_type=jnp.float32)).astype(jnp.bfloat16)
    atm_out = (atm_mid + jnp.dot(expanded, w_down, preferred_element_type=jnp.float32)).astype(jnp.bfloat16)
    fluxes = jnp.dot(atm_state.astype(jnp.float32), w_flux, precision=highest).T
    flux_picked = fluxes[:, flux_columns]
    flux_cells = lax.optimization_barrier(jnp.sum(flux_picked * flux_weights[None], axis=1))
    forcing = jnp.einsum('fab,fc->abc', flux_cells, w_flux_in, precision=highest)
    sea = wet_mask.astype(jnp.float32)[:, :, None]
    ocean_x = (sea * (ocean_state.astype(jnp.float32) + forcing)).astype(jnp.bfloat16)
    reach = KS // 2
    for ordinal in range(BLOCKS):
        padded = jnp.pad(ocean_x, ((0, 0), (reach, reach), (0, 0)), mode='wrap')
        padded = jnp.pad(padded, ((reach, reach), (0, 0), (0, 0)))
        conv = jnp.zeros((NLAT, NLON, C), jnp.float32) + dw_bias[ordinal]
        for row_tap in range(KS):
            for col_tap in range(KS):
                window = padded[row_tap:row_tap + NLAT, col_tap:col_tap + NLON].astype(jnp.float32)
                conv = conv + dw_kernel[ordinal, row_tap * KS + col_tap] * window
        onorm = layer_norm(conv, ocean_gain[ordinal], 1e-06).astype(jnp.bfloat16)
        grouped = onorm.reshape(NLAT // LAT_T, LAT_T * NLON, C)
        expand_now = w_expand[ordinal]
        reduce_now = w_reduce[ordinal]

        def pointwise(rows):
            grown = jax.nn.gelu(jnp.dot(rows, expand_now, preferred_element_type=jnp.float32)).astype(jnp.bfloat16)
            return jnp.dot(grown, reduce_now, preferred_element_type=jnp.float32)
        reduced = lax.map(pointwise, grouped).reshape(NLAT, NLON, C)
        ocean_x = (sea * (ocean_x.astype(jnp.float32) + layer_scale[ordinal] * reduced)).astype(jnp.bfloat16)
    return (atm_out, edge_out, ocean_x)
```

```python
import functools
import jax
import jax.numpy as jnp
from jax import lax
from jax.experimental import pallas as pl
from jax.experimental.pallas import tpu as pltpu
from jax.sharding import PartitionSpec as P

F32 = jnp.float32
BF16 = jnp.bfloat16


def iota(shape, axis):
    return lax.broadcasted_iota(jnp.int32, shape, axis)


def swap_blocks(parts):
    lane = iota(parts[0].shape, 1)
    upper = lane >= 64
    odd = (lane // 32) % 2 == 1
    first = []
    for low in range(2):
        a, b = parts[low], parts[low + 2]
        first.append((jnp.where(upper, pltpu.roll(b, 64, 1), a), jnp.where(upper, b, pltpu.roll(a, 64, 1))))
    out = [None] * 4
    for side in range(2):
        a, b = first[0][side], first[1][side]
        out[2 * side] = jnp.where(odd, pltpu.roll(b, 32, 1), a)
        out[2 * side + 1] = jnp.where(odd, b, pltpu.roll(a, 96, 1))
    return out


def order_matrix():
    row, col = iota((128, 128), 0), iota((128, 128), 1)
    return jnp.where(col == 8 * (row % 16) + row // 16, 1.0, 0.0)


def build_weights(block, kernel_ref, w_ref):
    eye = (iota((32, 256), 0) == iota((32, 256), 1) % 32)

    def body(tap, carry):
        rows = kernel_ref[pl.ds(tap * 7, 7), block]
        stack = jnp.concatenate([rows, jnp.zeros((17, 256), F32)], axis=0)
        shifted = [stack if j == 0 else pltpu.roll(stack, j, 0) for j in range(8)]
        for t in range(2):
            halves = []
            for h in range(2):
                halves.append(swap_blocks([shifted[4 * h + i][0:16, 128 * t : 128 * t + 128] for i in range(4)]))
            for u in range(4):
                line = jnp.concatenate([halves[0][u], halves[1][u]], axis=1)
                for n in range(16):
                    piece = jnp.where(eye, jnp.broadcast_to(line[n : n + 1], (32, 256)), 0.0)
                    w_ref[4 * t + u, pl.ds(tap * 512 + n * 32, 32)] = piece.astype(BF16)
        return carry

    lax.fori_loop(0, 7, body, 0)


def fill_rows(tile_of, west, east, xt_ref, row):
    first = iota((16, 256), 0) == 0
    last = iota((16, 256), 0) == 15
    plain = [tile_of(j) for j in range(8)]
    zero_view, one_view = [None] * 8, [None] * 8
    for p in range(8):
        if p < 3:
            data = plain[p + 5]
            one_view[p] = data
            edge = jnp.broadcast_to(west[p + 4 : p + 5], (16, 256))
            zero_view[p] = jnp.where(first, edge, pltpu.roll(data.astype(F32), 1, 0)).astype(BF16)
        else:
            data = plain[p - 3]
            zero_view[p] = data
            rolled = pltpu.roll(data.astype(F32), 15, 0)
            if p < 6:
                rolled = jnp.where(last, jnp.broadcast_to(east[p - 3 : p - 2], (16, 256)), rolled)
            one_view[p] = rolled.astype(BF16)
    for q, view in enumerate((zero_view, one_view)):
        for t in range(2):
            for h in range(2):
                done = swap_blocks([view[4 * h + i][:, 128 * t : 128 * t + 128] for i in range(4)])
                for u in range(4):
                    xt_ref[q, 4 * t + u, row, :, 128 * h : 128 * h + 128] = done[u]


def block_body(last, kernel_ref, bias_ref, gain_ref, scale_ref, up_ref, down_ref, mask_ref, x_ref, north_ref, south_ref,
               west_ref, east_ref, nw_ref, ne_ref, sw_ref, se_ref, out_ref, edge_ref, w_ref, xt_ref, conv_ref, stat_ref, rms_ref):
    block = 1 if last else 0
    build_weights(block, kernel_ref, w_ref)

    def interior(r, carry):
        at = pl.multiple_of(r * 8, 8)
        fill_rows(lambda j: x_ref[r, j], west_ref[pl.ds(at, 8)].astype(F32), east_ref[pl.ds(at, 8)].astype(F32), xt_ref, r + 3)
        return carry

    lax.fori_loop(0, 32, interior, 0, unroll=2)
    for k in range(3):
        fill_rows(lambda j: north_ref[k, j], nw_ref[8 + 8 * k : 16 + 8 * k].astype(F32), ne_ref[8 + 8 * k : 16 + 8 * k].astype(F32), xt_ref, k)
        fill_rows(lambda j: south_ref[k, j], sw_ref[8 * k : 8 * k + 8].astype(F32), se_ref[8 * k : 8 * k + 8].astype(F32), xt_ref, 35 + k)

    grouped = []
    lines = jnp.concatenate([bias_ref[block : block + 1]] + [gain_ref[block : block + 1]] * 7, axis=0)
    scale = scale_ref[block : block + 1]
    for t in range(2):
        part = lines[:, 128 * t : 128 * t + 128]
        grouped += [jnp.concatenate([v, v], axis=1) for v in swap_blocks([part] * 4)]

    for g in range(8):
        pieces = []
        for a in range(7):
            for q in range(2):
                pieces.append(xt_ref[q, g, a : a + 32].reshape(512, 256))
        acc = jnp.dot(jnp.concatenate(pieces, axis=1), w_ref[g], preferred_element_type=F32) + grouped[g][0:1]
        conv_ref[g] = acc
        stat_ref[...] = acc if g == 0 else stat_ref[...] + acc

    same = jnp.where(iota((256, 256), 0) // 32 == iota((256, 256), 1) // 32, 1.0 / 256, 0.0).astype(BF16)
    same2 = jnp.concatenate([same, same], axis=0)

    def spread(values):
        high = values.astype(BF16)
        low = (values - high.astype(F32)).astype(BF16)
        return jnp.dot(jnp.concatenate([high, low], axis=1), same2, preferred_element_type=F32)

    stat_ref[...] = spread(stat_ref[...])

    def squares(n, carry):
        at = pl.ds(pl.multiple_of(n * 64, 64), 64)
        mean = stat_ref[at]
        total = None
        for g in range(8):
            centre = conv_ref[g, at] - mean
            total = centre * centre if total is None else total + centre * centre
        rms_ref[at] = total
        return carry

    lax.fori_loop(0, 8, squares, 0)
    rms_ref[...] = lax.rsqrt(spread(rms_ref[...]) + 1e-6)
    order = order_matrix()
    ones = jnp.ones((128, 256), BF16)
    order_back = jnp.where(iota((128, 128), 0) == 8 * (iota((128, 128), 1) % 16) + iota((128, 128), 1) // 16, 1.0, 0.0).astype(BF16)

    def mlp(n, carry):
        at = pl.ds(pl.multiple_of(n * 64, 64), 64)
        mean, rms = stat_ref[at], rms_ref[at]
        norm = [((conv_ref[g, at] - mean) * rms * grouped[g][1:2]).astype(BF16) for g in range(8)]
        tiles = [[None] * 2 for _ in range(8)]
        for h in range(2):
            for t in range(2):
                done = swap_blocks([norm[4 * t + u][:, 128 * h : 128 * h + 128] for u in range(4)])
                for i in range(4):
                    tiles[4 * h + i][t] = done[i]
        full = [jnp.concatenate(pair, axis=1) for pair in tiles]
        rows = jnp.concatenate([full[j][16 * k : 16 * k + 16] for k in range(4) for j in range(8)], axis=0)
        wide = jnp.dot(rows, up_ref[block], preferred_element_type=F32)
        grown = jax.nn.gelu(wide).astype(BF16)
        small = jnp.dot(grown, down_ref[block], preferred_element_type=F32)
        picks = jnp.concatenate([order * mask_ref[pl.ds(4 * n + k, 1)].astype(F32) for k in range(4)], axis=0).astype(BF16)
        sea = jnp.dot(picks, ones, preferred_element_type=F32)
        base = x_ref[pl.ds(4 * n, 4)].reshape(512, 256).astype(F32)
        fresh = sea * (base + scale * small)
        fresh16 = fresh.astype(BF16)
        if last:
            for k in range(4):
                natural = jnp.dot(order_back, fresh16[128 * k : 128 * k + 128], preferred_element_type=F32)
                out_ref[4 * n + k] = natural.astype(BF16)
        else:
            out_ref[pl.ds(4 * n, 4)] = fresh16.reshape(4, 8, 16, 256)
            lines = []
            for k in range(4):
                lines += edge_lines(fresh[128 * k : 128 * k + 128])
            edge_ref[pl.ds(pl.multiple_of(32 * n, 32), 32)] = jnp.concatenate(lines, axis=0).astype(BF16)
        return carry

    lax.fori_loop(0, 8, mlp, 0, unroll=2)


def edge_lines(rows):
    at = (0, 16, 32, 48, 95, 111, 127, 111)
    return [rows[p : p + 1] for p in at]


def ocean_block(last, kernel, bias, gain, scale, up, down, mask, x, halo):
    def body(*refs):
        ins, rest = refs[:16], refs[16:]
        if last:
            out_ref, scratch = rest[0], rest[1:]
            block_body(True, *ins, out_ref, None, *scratch)
        else:
            block_body(False, *ins, rest[0], rest[1], *rest[2:])

    vm = pl.BlockSpec(memory_space=pltpu.VMEM)
    args = (kernel.transpose(1, 0, 2), bias, gain, scale, up, down, mask, x) + tuple(halo)
    specs_in = [vm] * len(args)
    if last:
        shapes = jax.ShapeDtypeStruct((32, 128, 256), BF16)
        specs = vm
    else:
        shapes = (jax.ShapeDtypeStruct((32, 8, 16, 256), BF16), jax.ShapeDtypeStruct((256, 256), BF16))
        specs = (vm, vm)
    return pl.pallas_call(
        body,
        out_shape=shapes,
        in_specs=specs_in,
        out_specs=specs,
        scratch_shapes=[
            pltpu.VMEM((8, 3584, 256), BF16),
            pltpu.VMEM((2, 8, 38, 16, 256), BF16),
            pltpu.VMEM((8, 512, 256), F32),
            pltpu.VMEM((512, 256), F32),
            pltpu.VMEM((512, 256), F32),
        ],
        compiler_params=pltpu.CompilerParams(vmem_limit_bytes=60 << 20),
        name="ocean_last" if last else "ocean_first",
    )(*args)


def vmem():
    return pl.BlockSpec(memory_space=pltpu.VMEM)


def anywhere():
    return pl.BlockSpec(memory_space=pl.ANY)


def split(values):
    high = values.astype(BF16)
    return high, (values - high.astype(F32)).astype(BF16)


def contract_last(a, b):
    return lax.dot_general(a, b, (((1,), (1,)), ((), ())), preferred_element_type=F32)


def contract_first(a, b):
    return lax.dot_general(a, b, (((0,), (0,)), ((), ())), preferred_element_type=F32)


def unit_norm(values, gain, epsilon):
    centre = values - jnp.mean(values, axis=-1, keepdims=True)
    spread = jnp.mean(centre * centre, axis=-1, keepdims=True)
    return centre * lax.rsqrt(spread + epsilon) * gain


def gather_kernel(state_ref, wflux_ref, fields_ref, table_ref, own_ref, send_sem, recv_sem, local_sem):
    me = lax.axis_index("lon")
    high, low = split(wflux_ref[...])
    both = contract_last(jnp.concatenate([high, low], axis=0), state_ref[...])
    fluxes = both[0:4] + both[4:8]
    own_ref[0:128] = fields_ref[...].astype(BF16)
    own_ref[128:144] = jnp.concatenate([fluxes, jnp.zeros((12, 128), F32)], axis=0).astype(BF16)
    barrier = pltpu.get_barrier_semaphore()
    for step in range(1, 16):
        pl.semaphore_signal(barrier, inc=1, device_id={"lon": lax.rem(me + step, 16)}, device_id_type=pl.DeviceIdType.MESH)
    pl.semaphore_wait(barrier, 15)
    copies = []
    for step in range(1, 16):
        copy = pltpu.make_async_remote_copy(
            src_ref=own_ref, dst_ref=table_ref.at[me], send_sem=send_sem.at[step], recv_sem=recv_sem.at[step],
            device_id={"lon": lax.rem(me + step, 16)}, device_id_type=pl.DeviceIdType.MESH)
        copy.start()
        copies.append(copy)
    mine = pltpu.make_async_copy(own_ref, table_ref.at[me], local_sem)
    mine.start()
    mine.wait()
    for copy in copies:
        copy.wait()


def band_gather(state, wflux, fields):
    return pl.pallas_call(
        gather_kernel,
        out_shape=jax.ShapeDtypeStruct((16, 144, 128), BF16),
        in_specs=[vmem()] * 3,
        out_specs=anywhere(),
        scratch_shapes=[pltpu.VMEM((144, 128), BF16), pltpu.SemaphoreType.DMA((16,)), pltpu.SemaphoreType.DMA((16,)), pltpu.SemaphoreType.DMA],
        compiler_params=pltpu.CompilerParams(collective_id=0, has_side_effects=True),
        name="band_gather",
    )(state, wflux, fields)


def halo_kernel(with_rims, *refs):
    if with_rims:
        x_ref, edge_ref, norm_ref = refs[:3]
        rims_ref = refs[11]
        halo, send_sem, recv_sem = refs[3:11], refs[12], refs[13]
    else:
        x_ref, edge_ref = refs[:2]
        halo, send_sem, recv_sem = refs[2:10], refs[10], refs[11]
    north, south, west, east, nw, ne, sw, se = halo
    band = lax.axis_index("comp") * 8 + lax.axis_index("lat")
    col = lax.axis_index("lon")

    def device(dr, dc):
        row = lax.rem(band + 16 + dr, 16)
        return {"comp": row // 8, "lat": lax.rem(row, 8), "lon": lax.rem(col + 16 + dc, 16)}

    around = [(dr, dc) for dr in (-1, 0, 1) for dc in (-1, 0, 1) if (dr, dc) != (0, 0)]
    barrier = pltpu.get_barrier_semaphore()
    for dr, dc in around:
        pl.semaphore_signal(barrier, inc=1, device_id=device(dr, dc), device_id_type=pl.DeviceIdType.MESH)
    pl.semaphore_wait(barrier, 8)
    top, bottom = edge_ref.at[pl.ds(0, 32)], edge_ref.at[pl.ds(224, 32)]
    moves = [
        (x_ref.at[pl.ds(0, 3)], south, -1, 0),
        (x_ref.at[pl.ds(29, 3)], north, 1, 0),
        (edge_ref, east, 0, -1),
        (edge_ref, west, 0, 1),
        (top, se, -1, -1),
        (top, sw, -1, 1),
        (bottom, ne, 1, -1),
        (bottom, nw, 1, 1),
    ]
    if with_rims:
        for dr, dc in around:
            slot = (1 - dr) * 3 + 1 - dc
            slot = slot - 1 if slot > 4 else slot
            moves.append((norm_ref.at[pl.ds(0, 64)], rims_ref.at[slot], dr, dc))
    copies = []
    for n, (source, target, dr, dc) in enumerate(moves):
        copy = pltpu.make_async_remote_copy(
            src_ref=source, dst_ref=target, send_sem=send_sem.at[n], recv_sem=recv_sem.at[n],
            device_id=device(dr, dc), device_id_type=pl.DeviceIdType.MESH)
        copy.start()
        copies.append(copy)
    for copy in copies:
        copy.wait()


def exchange(x, edge, normed=None):
    rims = normed is not None
    shapes = [jax.ShapeDtypeStruct((3, 8, 16, 256), BF16)] * 2 + [jax.ShapeDtypeStruct((256, 256), BF16)] * 2
    shapes += [jax.ShapeDtypeStruct((32, 256), BF16)] * 4
    args = [x, edge]
    if rims:
        shapes.append(jax.ShapeDtypeStruct((8, 64, 512), BF16))
        args.append(normed)
    count = 16 if rims else 8
    return pl.pallas_call(
        functools.partial(halo_kernel, rims),
        out_shape=tuple(shapes),
        in_specs=[anywhere()] * len(args),
        out_specs=tuple([anywhere()] * len(shapes)),
        scratch_shapes=[pltpu.SemaphoreType.DMA((count,)), pltpu.SemaphoreType.DMA((count,))],
        compiler_params=pltpu.CompilerParams(collective_id=1 if rims else 2, has_side_effects=True),
        name="exchange_first" if rims else "exchange_second",
    )(*args)


def front_kernel(table_ref, cols_ref, fluxw_ref, ocean_ref, mask_ref, wfin_ref, scols_ref, sw_ref, state_ref, wsurf_ref, gain_ref,
                 x_ref, edge_ref, atm_ref, norm_ref):
    pairs = []
    for p in range(8):
        pairs.append(jnp.concatenate([table_ref[2 * p, 128:132], table_ref[2 * p + 1, 128:132]], axis=0))
    small = jnp.concatenate(pairs, axis=0)
    node = iota((128, 128), 0)
    half = iota((8, 128), 0) // 4
    wide = jnp.concatenate([wfin_ref[...], wfin_ref[...]], axis=0)
    whigh, wlow = split(wide)
    zero8 = jnp.zeros((8, 256), BF16)
    right = jnp.concatenate([
        jnp.concatenate([whigh, zero8], axis=1), jnp.concatenate([whigh, zero8], axis=1),
        jnp.concatenate([wlow, zero8], axis=1), jnp.concatenate([zero8, jnp.ones((8, 256), BF16)], axis=1)], axis=0)
    order = order_matrix().astype(BF16)
    top_row = iota((8, 128), 0) == 0

    def row(r, carry):
        ids = [cols_ref[k, pl.ds(r, 1)] for k in range(4)]
        hots = [jnp.where(node == (i & 127), 1.0, 0.0).astype(BF16) for i in ids]
        picked = jnp.dot(small, jnp.concatenate(hots, axis=1), preferred_element_type=F32)
        cell = None
        for k in range(4):
            part = (ids[k] >> 7) & 15
            level = part >> 1
            total = None
            for p in range(8):
                term = jnp.where(level == p, picked[8 * p : 8 * p + 8, 128 * k : 128 * k + 128], 0.0)
                total = term if total is None else total + term
            total = jnp.where(half == (part & 1), total, 0.0) * fluxw_ref[k, pl.ds(r, 1)]
            cell = total if cell is None else cell + total
        high, low = split(cell)
        sea = jnp.where(top_row, mask_ref[pl.ds(r, 1)].astype(F32), 0.0).astype(BF16)
        both = contract_first(jnp.concatenate([high, low, high, sea], axis=0), right)
        fresh = both[:, 256:512] * (ocean_ref[r].astype(F32) + both[:, 0:256])
        fresh16 = fresh.astype(BF16)
        x_ref[r] = jnp.dot(order, fresh16, preferred_element_type=F32).astype(BF16).reshape(8, 16, 256)
        line = jnp.concatenate([fresh[0:4], fresh[125:128], fresh[127:128]], axis=0)
        edge_ref[pl.ds(pl.multiple_of(r * 8, 8), 8)] = line.astype(BF16)
        return carry

    lax.fori_loop(0, 32, row, 0)

    ids = jnp.concatenate([scols_ref[k : k + 1] for k in range(4)], axis=1)
    cell = ids & 2047
    level = (ids >> 11) & 31
    spot = iota((128, 512), 0)
    hots, tabs = [], []
    for p in range(16):
        hots.append(jnp.where(spot + 128 * p == cell, 1.0, 0.0).astype(BF16))
        tabs.append(table_ref[p, 0:128])
    picked = jnp.dot(jnp.concatenate(tabs, axis=1), jnp.concatenate(hots, axis=0), preferred_element_type=F32)
    weight = jnp.concatenate([sw_ref[k : k + 1] for k in range(4)], axis=1)
    chosen = jnp.where(iota((32, 512), 0) == level, weight, 0.0)
    sums = []
    for s in range(4):
        term = jnp.sum(picked[32 * s : 32 * s + 32] * chosen, axis=0, keepdims=True)
        sums.append(term[:, 0:128] + term[:, 128:256] + term[:, 256:384] + term[:, 384:512])
    nodes = jnp.concatenate(sums + [jnp.zeros((4, 128), F32)], axis=0)
    high, low = split(nodes)
    whigh, wlow = split(jnp.concatenate([wsurf_ref[...], jnp.zeros((4, 512), F32)], axis=0))
    zeros = jnp.zeros((8, 128), BF16)
    lift = contract_first(jnp.concatenate([high, low, high, zeros], axis=0), jnp.concatenate([whigh, whigh, wlow, jnp.zeros((8, 512), BF16)], axis=0))
    atm_in = state_ref[...].astype(F32) + lift
    atm_ref[...] = atm_in
    norm_ref[...] = unit_norm(atm_in, gain_ref[...], 1e-5).astype(BF16)


def front(*args):
    return pl.pallas_call(
        front_kernel,
        out_shape=(
            jax.ShapeDtypeStruct((32, 8, 16, 256), BF16),
            jax.ShapeDtypeStruct((256, 256), BF16),
            jax.ShapeDtypeStruct((128, 512), F32),
            jax.ShapeDtypeStruct((128, 512), BF16),
        ),
        in_specs=[vmem()] * len(args),
        out_specs=tuple([vmem()] * 4),
        compiler_params=pltpu.CompilerParams(vmem_limit_bytes=60 << 20),
        name="front",
    )(*args)


def silu(values):
    return values * jax.nn.sigmoid(values)


def atmosphere_kernel(norm_ref, rims_ref, atm_ref, edges_ref, near_ref, degree_ref, wq_ref, wk_ref, wv_ref, wo_ref, win_ref, wsrc_ref,
                      wdst_ref, wout_ref, wbias_ref, gain_ref, up_ref, down_ref, out_ref, edge_out_ref):
    band = lax.axis_index("comp") * 8 + lax.axis_index("lat")
    col = lax.axis_index("lon")
    ids = near_ref[...]
    part, inside = ids >> 7, ids & 127
    down = (part >> 4) - band
    right = (((part & 15) - col + 1) & 15) - 1
    spot = (down + 1) * 3 + right + 1
    spot = spot - jnp.where(spot > 4, 1, 0)
    at = jnp.where((down == 0) & (right == 0), inside, 128 + spot * 64 + inside)
    info = jnp.concatenate([at, degree_ref[...], degree_ref[...]], axis=0).astype(F32)
    info = info.T
    table = jnp.concatenate([norm_ref[...], rims_ref[...]], axis=0)
    lane = iota((128, 640), 1).astype(F32)
    hots = [jnp.where(lane == info[:, k : k + 1], 1.0, 0.0).astype(BF16) for k in range(6)]
    near = jnp.dot(jnp.concatenate(hots, axis=0), table, preferred_element_type=F32).astype(BF16)
    keys = jnp.dot(near, wk_ref[...], preferred_element_type=F32).astype(BF16)
    values = jnp.dot(near, wv_ref[...], preferred_element_type=F32).astype(BF16)
    far = jnp.dot(near, wdst_ref[...], preferred_element_type=F32).astype(BF16)
    query = jnp.dot(norm_ref[...], wq_ref[...], preferred_element_type=F32).astype(BF16).astype(F32)
    own = jnp.dot(norm_ref[...], wsrc_ref[...], preferred_element_type=F32)
    edges = edges_ref[...].reshape(768, 512)
    before = jnp.dot(edges, win_ref[...], preferred_element_type=F32)
    hidden = []
    for k in range(6):
        rows = slice(128 * k, 128 * k + 128)
        hidden.append(silu(before[rows] + own + far[rows].astype(F32)).astype(BF16))
    edge_sum = edges.astype(F32) + jnp.dot(jnp.concatenate(hidden, axis=0), wout_ref[...], preferred_element_type=F32)
    edge_out_ref[...] = edge_sum.astype(BF16).reshape(6, 128, 512)
    head = jnp.where(iota((8, 512), 0) == iota((8, 512), 1) // 64, 1.0, 0.0)
    scaled = (head * 0.125).astype(BF16)
    bhigh, blow = split(wbias_ref[...])
    mixer = jnp.concatenate([scaled, scaled, bhigh, bhigh, blow], axis=1)
    scores = []
    for k in range(6):
        rows = slice(128 * k, 128 * k + 128)
        qhigh, qlow = split(query * keys[rows].astype(F32))
        ehigh, elow = split(edge_sum[rows])
        score = contract_last(jnp.concatenate([qhigh, qlow, ehigh, elow, ehigh], axis=1), mixer)
        scores.append(jnp.where(info[:, 6:7] > k, score, -1e30))
    most = functools.reduce(jnp.maximum, scores)
    powers = [jnp.exp(score - most) for score in scores]
    total = functools.reduce(jnp.add, powers)
    attended = None
    for k in range(6):
        weight = (powers[k] / total).astype(BF16)
        spread = jnp.dot(weight, head.astype(BF16), preferred_element_type=F32)
        term = spread * values[128 * k : 128 * k + 128].astype(F32)
        attended = term if attended is None else attended + term
    middle = atm_ref[...] + jnp.dot(attended.astype(BF16), wo_ref[...], preferred_element_type=F32)
    normed2 = unit_norm(middle, gain_ref[...], 1e-5).astype(BF16)
    expanded = silu(jnp.dot(normed2, up_ref[...], preferred_element_type=F32)).astype(BF16)
    out_ref[...] = (middle + jnp.dot(expanded, down_ref[...], preferred_element_type=F32)).astype(BF16)


def atmosphere(*args):
    return pl.pallas_call(
        atmosphere_kernel,
        out_shape=(jax.ShapeDtypeStruct((128, 512), BF16), jax.ShapeDtypeStruct((6, 128, 512), BF16)),
        in_specs=[vmem()] * len(args),
        out_specs=(vmem(), vmem()),
        compiler_params=pltpu.CompilerParams(vmem_limit_bytes=60 << 20),
        name="atmosphere",
    )(*args)


def local(atm_state, edge_state, neighbours, degree, surface_fields, ocean_state, wet_mask, flux_columns, flux_weights,
          surface_columns, surface_weights, w_surface, w_flux, ln1_gain, w_query, w_key, w_value, w_out, w_edge_in, w_edge_src,
          w_edge_dst, w_edge_out, w_bias, ln2_gain, w_up, w_down, w_flux_in, dw_kernel, dw_bias, ocean_gain, w_expand, w_reduce,
          layer_scale):
    table = band_gather(atm_state, w_flux.T, surface_fields.reshape(128, 128))
    x, edge, atm_in, normed = front(table, flux_columns, flux_weights, ocean_state, wet_mask, w_flux_in, surface_columns,
                                    surface_weights, atm_state, w_surface, ln1_gain.reshape(1, 512))
    *halo, rims = exchange(x, edge, normed)
    x, edge = ocean_block(False, dw_kernel, dw_bias, ocean_gain, layer_scale, w_expand, w_reduce, wet_mask, x, halo)
    halo = exchange(x, edge)
    ocean_out = ocean_block(True, dw_kernel, dw_bias, ocean_gain, layer_scale, w_expand, w_reduce, wet_mask, x, halo)
    atm_out, edge_out = atmosphere(
        normed, rims.reshape(512, 512), atm_in, edge_state.transpose(1, 0, 2), neighbours.T, degree.reshape(1, 128), w_query, w_key,
        w_value, w_out, w_edge_in, w_edge_src, w_edge_dst, w_edge_out, w_bias.T, ln2_gain.reshape(1, 512), w_up, w_down)
    return atm_out, edge_out.transpose(1, 0, 2), ocean_out


def solution(mesh):
    whole, rows = ("comp", "lat", "lon"), ("comp", "lat")
    in_specs = (
        P(whole, None), P(whole, None, None), P(whole, None), P(whole), P(None, rows, "lon"), P(rows, "lon", None), P(rows, "lon"),
        P(None, rows, "lon"), P(None, rows, "lon"), P(None, whole), P(None, whole)) + (P(),) * 22
    out_specs = (P(whole, None), P(whole, None, None), P(rows, "lon", None))
    return jax.shard_map(local, mesh=mesh, in_specs=in_specs, out_specs=out_specs, check_vma=False)
```

```python
import functools
import jax
import jax.numpy as jnp
from jax import lax
from jax.experimental import pallas as pl
from jax.experimental.pallas import tpu as pltpu
from jax.sharding import PartitionSpec as P

F32 = jnp.float32
BF16 = jnp.bfloat16


def iota(shape, axis):
    return lax.broadcasted_iota(jnp.int32, shape, axis)


def swap_blocks(parts):
    lane = iota(parts[0].shape, 1)
    upper = lane >= 64
    odd = (lane // 32) % 2 == 1
    first = []
    for low in range(2):
        a, b = parts[low], parts[low + 2]
        first.append((jnp.where(upper, pltpu.roll(b, 64, 1), a), jnp.where(upper, b, pltpu.roll(a, 64, 1))))
    out = [None] * 4
    for side in range(2):
        a, b = first[0][side], first[1][side]
        out[2 * side] = jnp.where(odd, pltpu.roll(b, 32, 1), a)
        out[2 * side + 1] = jnp.where(odd, b, pltpu.roll(a, 96, 1))
    return out


def order_matrix():
    row, col = iota((128, 128), 0), iota((128, 128), 1)
    return jnp.where(col == 8 * (row % 16) + row // 16, 1.0, 0.0)


def build_weights(block, kernel_ref, w_ref):
    eye = (iota((32, 256), 0) == iota((32, 256), 1) % 32)

    def body(tap, carry):
        rows = kernel_ref[pl.ds(tap * 7, 7), block]
        stack = jnp.concatenate([rows, jnp.zeros((17, 256), F32)], axis=0)
        shifted = [stack if j == 0 else pltpu.roll(stack, j, 0) for j in range(8)]
        for t in range(2):
            halves = []
            for h in range(2):
                halves.append(swap_blocks([shifted[4 * h + i][0:16, 128 * t : 128 * t + 128] for i in range(4)]))
            for u in range(4):
                line = jnp.concatenate([halves[0][u], halves[1][u]], axis=1)
                for n in range(16):
                    piece = jnp.where(eye, jnp.broadcast_to(line[n : n + 1], (32, 256)), 0.0)
                    w_ref[4 * t + u, pl.ds(tap * 512 + n * 32, 32)] = piece.astype(BF16)
        return carry

    lax.fori_loop(0, 7, body, 0)


def fill_rows(tile_of, west, east, xt_ref, row):
    first = iota((16, 256), 0) == 0
    last = iota((16, 256), 0) == 15
    plain = [tile_of(j) for j in range(8)]
    zero_view, one_view = [None] * 8, [None] * 8
    for p in range(8):
        if p < 3:
            data = plain[p + 5]
            one_view[p] = data
            edge = jnp.broadcast_to(west(p), (16, 256))
            zero_view[p] = jnp.where(first, edge, pltpu.roll(data.astype(F32), 1, 0)).astype(BF16)
        else:
            data = plain[p - 3]
            zero_view[p] = data
            rolled = pltpu.roll(data.astype(F32), 15, 0)
            if p < 6:
                rolled = jnp.where(last, jnp.broadcast_to(east(p - 3), (16, 256)), rolled)
            one_view[p] = rolled.astype(BF16)
    for q, view in enumerate((zero_view, one_view)):
        for t in range(2):
            for h in range(2):
                done = swap_blocks([view[4 * h + i][:, 128 * t : 128 * t + 128] for i in range(4)])
                for u in range(4):
                    xt_ref[q, 4 * t + u, row, :, 128 * h : 128 * h + 128] = done[u]


def block_body(last, kernel_ref, bias_ref, gain_ref, scale_ref, up_ref, down_ref, mask_ref, x_ref, arrived, halo,
               out_ref, edge_ref, w_ref, xt_ref, conv_ref, stat_ref, rms_ref, side_ref, corner_ref, lines_ref):
    block = 1 if last else 0
    build_weights(block, kernel_ref, w_ref)
    arrived()
    north_ref, south_ref, west_ref, east_ref, nw_ref, ne_ref, sw_ref, se_ref = halo
    side_ref[0:3] = west_ref[...].astype(F32)
    side_ref[3:6] = east_ref[...].astype(F32)
    for n, ref in enumerate((nw_ref, ne_ref, sw_ref, se_ref)):
        corner_ref[3 * n : 3 * n + 3] = ref[...].astype(F32)

    def interior(r, carry):
        fill_rows(lambda j: x_ref[r, j], lambda p: side_ref[p, pl.ds(r, 1)], lambda p: side_ref[3 + p, pl.ds(r, 1)], xt_ref, r + 3)
        return carry

    lax.fori_loop(0, 32, interior, 0, unroll=2)

    def outer(k, carry):
        fill_rows(lambda j: north_ref[k, j], lambda p: corner_ref[p, pl.ds(13 + k, 1)], lambda p: corner_ref[3 + p, pl.ds(13 + k, 1)], xt_ref, k)
        fill_rows(lambda j: south_ref[k, j], lambda p: corner_ref[6 + p, pl.ds(k, 1)], lambda p: corner_ref[9 + p, pl.ds(k, 1)], xt_ref, 35 + k)
        return carry

    lax.fori_loop(0, 3, outer, 0)

    grouped = []
    lines = jnp.concatenate([bias_ref[block : block + 1]] + [gain_ref[block : block + 1]] * 7, axis=0)
    scale = scale_ref[block : block + 1]
    for t in range(2):
        part = lines[:, 128 * t : 128 * t + 128]
        grouped += [jnp.concatenate([v, v], axis=1) for v in swap_blocks([part] * 4)]

    for g in range(8):
        pieces = []
        for a in range(7):
            for q in range(2):
                pieces.append(xt_ref[q, g, a : a + 32].reshape(512, 256))
        acc = jnp.dot(jnp.concatenate(pieces, axis=1), w_ref[g], preferred_element_type=F32) + grouped[g][0:1]
        conv_ref[g] = acc
        stat_ref[...] = acc if g == 0 else stat_ref[...] + acc

    same = jnp.where(iota((256, 256), 0) // 32 == iota((256, 256), 1) // 32, 1.0 / 256, 0.0).astype(BF16)
    same2 = jnp.concatenate([same, same], axis=0)

    def spread(values):
        high = values.astype(BF16)
        low = (values - high.astype(F32)).astype(BF16)
        return jnp.dot(jnp.concatenate([high, low], axis=1), same2, preferred_element_type=F32)

    stat_ref[...] = spread(stat_ref[...])

    def squares(n, carry):
        at = pl.ds(pl.multiple_of(n * 64, 64), 64)
        mean = stat_ref[at]
        total = None
        for g in range(8):
            centre = conv_ref[g, at] - mean
            total = centre * centre if total is None else total + centre * centre
        rms_ref[at] = total
        return carry

    lax.fori_loop(0, 8, squares, 0)
    rms_ref[...] = lax.rsqrt(spread(rms_ref[...]) + 1e-6)
    order = order_matrix()
    ones = jnp.ones((128, 256), BF16)
    order_back = jnp.where(iota((128, 128), 0) == 8 * (iota((128, 128), 1) % 16) + iota((128, 128), 1) // 16, 1.0, 0.0).astype(BF16)

    def mlp(n, carry):
        at = pl.ds(pl.multiple_of(n * 64, 64), 64)
        mean, rms = stat_ref[at], rms_ref[at]
        norm = [((conv_ref[g, at] - mean) * rms * grouped[g][1:2]).astype(BF16) for g in range(8)]
        tiles = [[None] * 2 for _ in range(8)]
        for h in range(2):
            for t in range(2):
                done = swap_blocks([norm[4 * t + u][:, 128 * h : 128 * h + 128] for u in range(4)])
                for i in range(4):
                    tiles[4 * h + i][t] = done[i]
        full = [jnp.concatenate(pair, axis=1) for pair in tiles]
        rows = jnp.concatenate([full[j][16 * k : 16 * k + 16] for k in range(4) for j in range(8)], axis=0)
        wide = jnp.dot(rows, up_ref[block], preferred_element_type=F32)
        grown = jax.nn.gelu(wide).astype(BF16)
        small = jnp.dot(grown, down_ref[block], preferred_element_type=F32)
        picks = jnp.concatenate([order * mask_ref[pl.ds(4 * n + k, 1)].astype(F32) for k in range(4)], axis=0).astype(BF16)
        sea = jnp.dot(picks, ones, preferred_element_type=F32)
        base = x_ref[pl.ds(4 * n, 4)].reshape(512, 256).astype(F32)
        fresh = sea * (base + scale * small)
        fresh16 = fresh.astype(BF16)
        if last:
            for k in range(4):
                natural = jnp.dot(order_back, fresh16[128 * k : 128 * k + 128], preferred_element_type=F32)
                out_ref[4 * n + k] = natural.astype(BF16)
        else:
            out_ref[pl.ds(4 * n, 4)] = fresh16.reshape(4, 8, 16, 256)
            for k in range(4):
                keep_edges(lines_ref, 4 * n + k, fresh[128 * k : 128 * k + 128], (0, 16, 32, 95, 111, 127))
        return carry

    lax.fori_loop(0, 8, mlp, 0, unroll=2)
    if not last:
        edge_ref[...] = lines_ref[...].astype(BF16)


def keep_edges(lines_ref, r, rows, at):
    for n, p in enumerate(at):
        lines_ref[n, pl.ds(r, 1)] = rows[p : p + 1]


def vmem():
    return pl.BlockSpec(memory_space=pltpu.VMEM)


def anywhere():
    return pl.BlockSpec(memory_space=pl.ANY)


def split(values):
    high = values.astype(BF16)
    return high, (values - high.astype(F32)).astype(BF16)


def contract_last(a, b):
    return lax.dot_general(a, b, (((1,), (1,)), ((), ())), preferred_element_type=F32)


def contract_first(a, b):
    return lax.dot_general(a, b, (((0,), (0,)), ((), ())), preferred_element_type=F32)


def unit_norm(values, gain, epsilon):
    centre = values - jnp.mean(values, axis=-1, keepdims=True)
    spread = jnp.mean(centre * centre, axis=-1, keepdims=True)
    return centre * lax.rsqrt(spread + epsilon) * gain


AROUND = [(dr, dc) for dr in (-1, 0, 1) for dc in (-1, 0, 1) if (dr, dc) != (0, 0)]
HALO = [((3, 8, 16, 256), BF16)] * 2 + [((3, 32, 256), BF16)] * 2 + [((3, 16, 256), BF16)] * 4
BLOCK_SCRATCH = [
    ((8, 3584, 256), BF16), ((2, 8, 38, 16, 256), BF16), ((8, 512, 256), F32), ((512, 256), F32), ((512, 256), F32),
    ((6, 32, 256), F32), ((12, 16, 256), F32), ((6, 32, 256), F32)]


def greet(devices):
    barrier = pltpu.get_barrier_semaphore()
    for device in devices:
        pl.semaphore_signal(barrier, inc=1, device_id=device, device_id_type=pl.DeviceIdType.MESH)
    pl.semaphore_wait(barrier, len(devices))


def neighbour(dr, dc):
    band = lax.axis_index("comp") * 8 + lax.axis_index("lat")
    row = lax.rem(band + 16 + dr, 16)
    return {"comp": row // 8, "lat": lax.rem(row, 8), "lon": lax.rem(lax.axis_index("lon") + 16 + dc, 16)}


def send(source, target, send_sem, recv_sem, device):
    copy = pltpu.make_async_remote_copy(
        src_ref=source, dst_ref=target, send_sem=send_sem, recv_sem=recv_sem, device_id=device, device_id_type=pl.DeviceIdType.MESH)
    copy.start()
    return copy


def start_halo(x_ref, edge_ref, halo, send_sem, recv_sem):
    north, south, west, east, nw, ne, sw, se = halo
    left, right = edge_ref.at[pl.ds(0, 3)], edge_ref.at[pl.ds(3, 3)]
    top, bottom = pl.ds(0, 16), pl.ds(16, 16)
    moves = [
        (x_ref.at[pl.ds(0, 3)], south, -1, 0), (x_ref.at[pl.ds(29, 3)], north, 1, 0), (left, east, 0, -1), (right, west, 0, 1),
        (edge_ref.at[pl.ds(0, 3), top], se, -1, -1), (edge_ref.at[pl.ds(3, 3), top], sw, -1, 1),
        (edge_ref.at[pl.ds(0, 3), bottom], ne, 1, -1), (edge_ref.at[pl.ds(3, 3), bottom], nw, 1, 1)]
    return [
        send(source, target, send_sem.at[n], recv_sem.at[n], neighbour(dr, dc))
        for n, (source, target, dr, dc) in enumerate(moves)]


def first_kernel(*refs):
    ins, x_ref, edge_ref, norm_ref = refs[:7], refs[7], refs[8], refs[9]
    out_ref, line_ref, rims_ref = refs[10:13]
    scratch, halo = refs[13:21], refs[21:29]
    send_sem, recv_sem = refs[29], refs[30]
    greet([neighbour(dr, dc) for dr, dc in AROUND])
    copies = start_halo(x_ref, edge_ref, halo, send_sem, recv_sem)
    rims = []
    for n, (dr, dc) in enumerate(AROUND):
        slot = (1 - dr) * 3 + 1 - dc
        slot = slot - 1 if slot > 4 else slot
        rims.append(send(norm_ref.at[pl.ds(0, 64)], rims_ref.at[slot], send_sem.at[8 + n], recv_sem.at[8 + n], neighbour(dr, dc)))

    def arrived():
        for copy in copies:
            copy.wait()

    block_body(False, *ins, x_ref, arrived, halo, out_ref, line_ref, *scratch)
    for copy in rims:
        copy.wait()


def ocean_first(*args):
    scratch = [pltpu.VMEM(*item) for item in BLOCK_SCRATCH + HALO] + [pltpu.SemaphoreType.DMA((16,))] * 2
    return pl.pallas_call(
        first_kernel,
        out_shape=(
            jax.ShapeDtypeStruct((32, 8, 16, 256), BF16), jax.ShapeDtypeStruct((6, 32, 256), BF16),
            jax.ShapeDtypeStruct((8, 64, 512), BF16)),
        in_specs=[vmem()] * len(args),
        out_specs=(vmem(), vmem(), anywhere()),
        scratch_shapes=scratch,
        compiler_params=pltpu.CompilerParams(vmem_limit_bytes=60 << 20, collective_id=1, has_side_effects=True),
        name="ocean_first",
    )(*args)


def last_kernel(*refs):
    ins, x_ref, halo, out_ref, scratch = refs[:7], refs[7], refs[8:16], refs[16], refs[17:]
    block_body(True, *ins, x_ref, lambda: None, halo, out_ref, None, *scratch)


def ocean_last(*args):
    return pl.pallas_call(
        last_kernel,
        out_shape=jax.ShapeDtypeStruct((32, 128, 256), BF16),
        in_specs=[vmem()] * len(args),
        out_specs=vmem(),
        scratch_shapes=[pltpu.VMEM(*item) for item in BLOCK_SCRATCH],
        compiler_params=pltpu.CompilerParams(vmem_limit_bytes=60 << 20),
        name="ocean_last",
    )(*args)


def front_kernel(wflux_ref, fields_ref, cols_ref, fluxw_ref, ocean_ref, mask_ref, wfin_ref, scols_ref, sw_ref, state_ref, wsurf_ref,
                 gain_ref, x_ref, edge_ref, atm_ref, norm_ref, flux_own, field_own, flux_tab, field_tab, lines_ref,
                 flux_send, flux_recv, field_send, field_recv, pass_send, pass_recv):
    me = lax.axis_index("lon")
    side, deep = me // 8, lax.rem(me, 8)
    partner = {"lon": lax.rem(me + 8, 16)}
    high, low = split(wflux_ref[...])
    both = contract_last(jnp.concatenate([high, low], axis=0), state_ref[...])
    fluxes = jnp.concatenate([both[0:4] + both[4:8], jnp.zeros((12, 128), F32)], axis=0).astype(BF16)
    fields = fields_ref[...].astype(BF16)
    flux_own[...] = fluxes
    field_own[...] = fields
    flux_tab[me] = fluxes
    field_tab[me] = fields
    greet([{"lon": lax.rem(me + step, 16)} for step in range(1, 16)])
    small_copies = [
        send(flux_own, flux_tab.at[me], flux_send.at[step], flux_recv.at[step], {"lon": lax.rem(me + step, 16)})
        for step in range(1, 16)]
    field_copies = [
        send(field_own, field_tab.at[me], field_send.at[step], field_recv.at[step], {"lon": side * 8 + lax.rem(deep + step, 8)})
        for step in range(1, 8)]
    pass_copies = [send(field_own, field_tab.at[me], pass_send.at[0], pass_recv.at[0], partner)]
    for copy in small_copies:
        copy.wait()

    pairs = []
    for p in range(8):
        pairs.append(jnp.concatenate([flux_tab[2 * p, 0:4], flux_tab[2 * p + 1, 0:4]], axis=0))
    small = jnp.concatenate(pairs, axis=0)
    node = iota((128, 128), 0)
    half = iota((8, 128), 0) // 4
    wide = jnp.concatenate([wfin_ref[...], wfin_ref[...]], axis=0)
    whigh, wlow = split(wide)
    zero8 = jnp.zeros((8, 256), BF16)
    right = jnp.concatenate([
        jnp.concatenate([whigh, zero8], axis=1), jnp.concatenate([whigh, zero8], axis=1),
        jnp.concatenate([wlow, zero8], axis=1), jnp.concatenate([zero8, jnp.ones((8, 256), BF16)], axis=1)], axis=0)
    order = order_matrix().astype(BF16)
    top_row = iota((8, 128), 0) == 0

    def row(r, carry):
        ids = [cols_ref[k, pl.ds(r, 1)] for k in range(4)]
        hots = [jnp.where(node == (i & 127), 1.0, 0.0).astype(BF16) for i in ids]
        picked = jnp.dot(small, jnp.concatenate(hots, axis=1), preferred_element_type=F32)
        cell = None
        for k in range(4):
            part = (ids[k] >> 7) & 15
            level = part >> 1
            total = None
            for p in range(8):
                term = jnp.where(level == p, picked[8 * p : 8 * p + 8, 128 * k : 128 * k + 128], 0.0)
                total = term if total is None else total + term
            total = jnp.where(half == (part & 1), total, 0.0) * fluxw_ref[k, pl.ds(r, 1)]
            cell = total if cell is None else cell + total
        high, low = split(cell)
        sea = jnp.where(top_row, mask_ref[pl.ds(r, 1)].astype(F32), 0.0).astype(BF16)
        both = contract_first(jnp.concatenate([high, low, high, sea], axis=0), right)
        fresh = both[:, 256:512] * (ocean_ref[r].astype(F32) + both[:, 0:256])
        fresh16 = fresh.astype(BF16)
        x_ref[r] = jnp.dot(order, fresh16, preferred_element_type=F32).astype(BF16).reshape(8, 16, 256)
        keep_edges(lines_ref, r, fresh, (0, 1, 2, 125, 126, 127))
        return carry

    lax.fori_loop(0, 16, row, 0, unroll=2)
    for step in range(1, 8):
        field_copies[step - 1].wait()
        block = field_tab.at[side * 8 + lax.rem(deep + 8 - step, 8)]
        pass_copies.append(send(block, block, pass_send.at[step], pass_recv.at[step], partner))
    lax.fori_loop(16, 32, row, 0, unroll=2)
    edge_ref[...] = lines_ref[...].astype(BF16)
    for copy in pass_copies:
        copy.wait()

    ids = jnp.concatenate([scols_ref[k : k + 1] for k in range(4)], axis=1)
    cell = ids & 2047
    level = (ids >> 11) & 31
    spot = iota((128, 512), 0)
    hots, tabs = [], []
    for p in range(16):
        hots.append(jnp.where(spot + 128 * p == cell, 1.0, 0.0).astype(BF16))
        tabs.append(field_tab[p])
    picked = jnp.dot(jnp.concatenate(tabs, axis=1), jnp.concatenate(hots, axis=0), preferred_element_type=F32)
    weight = jnp.concatenate([sw_ref[k : k + 1] for k in range(4)], axis=1)
    chosen = jnp.where(iota((32, 512), 0) == level, weight, 0.0)
    sums = []
    for s in range(4):
        term = jnp.sum(picked[32 * s : 32 * s + 32] * chosen, axis=0, keepdims=True)
        sums.append(term[:, 0:128] + term[:, 128:256] + term[:, 256:384] + term[:, 384:512])
    nodes = jnp.concatenate(sums + [jnp.zeros((4, 128), F32)], axis=0)
    high, low = split(nodes)
    whigh, wlow = split(jnp.concatenate([wsurf_ref[...], jnp.zeros((4, 512), F32)], axis=0))
    zeros = jnp.zeros((8, 128), BF16)
    lift = contract_first(jnp.concatenate([high, low, high, zeros], axis=0), jnp.concatenate([whigh, whigh, wlow, jnp.zeros((8, 512), BF16)], axis=0))
    atm_in = state_ref[...].astype(F32) + lift
    atm_ref[...] = atm_in
    norm_ref[...] = unit_norm(atm_in, gain_ref[...], 1e-5).astype(BF16)


def front(*args):
    return pl.pallas_call(
        front_kernel,
        out_shape=(
            jax.ShapeDtypeStruct((32, 8, 16, 256), BF16),
            jax.ShapeDtypeStruct((6, 32, 256), BF16),
            jax.ShapeDtypeStruct((128, 512), F32),
            jax.ShapeDtypeStruct((128, 512), BF16),
        ),
        in_specs=[vmem()] * len(args),
        out_specs=tuple([vmem()] * 4),
        scratch_shapes=[
            pltpu.VMEM((16, 128), BF16), pltpu.VMEM((128, 128), BF16), pltpu.VMEM((16, 16, 128), BF16), pltpu.VMEM((16, 128, 128), BF16),
            pltpu.VMEM((6, 32, 256), F32)] + [pltpu.SemaphoreType.DMA((16,))] * 2 + [pltpu.SemaphoreType.DMA((8,))] * 4,
        compiler_params=pltpu.CompilerParams(vmem_limit_bytes=60 << 20, collective_id=0, has_side_effects=True),
        name="front",
    )(*args)


def silu(values):
    return values * jax.nn.sigmoid(values)


def atmosphere_kernel(norm_ref, rims_ref, atm_ref, edges_ref, near_ref, degree_ref, wq_ref, wk_ref, wv_ref, wo_ref, win_ref, wsrc_ref,
                      wdst_ref, wout_ref, wbias_ref, gain_ref, up_ref, down_ref, x_ref, line_ref, out_ref, edge_out_ref, *rest):
    greet([neighbour(dr, dc) for dr, dc in AROUND])
    copies = start_halo(x_ref, line_ref, rest[:8], rest[8], rest[9])
    band = lax.axis_index("comp") * 8 + lax.axis_index("lat")
    col = lax.axis_index("lon")
    ids = near_ref[...]
    part, inside = ids >> 7, ids & 127
    down = (part >> 4) - band
    right = (((part & 15) - col + 1) & 15) - 1
    spot = (down + 1) * 3 + right + 1
    spot = spot - jnp.where(spot > 4, 1, 0)
    at = jnp.where((down == 0) & (right == 0), inside, 128 + spot * 64 + inside)
    info = jnp.concatenate([at, degree_ref[...], degree_ref[...]], axis=0).astype(F32)
    info = info.T
    table = jnp.concatenate([norm_ref[...], rims_ref[...]], axis=0)
    lane = iota((128, 640), 1).astype(F32)
    hots = [jnp.where(lane == info[:, k : k + 1], 1.0, 0.0).astype(BF16) for k in range(6)]
    near = jnp.dot(jnp.concatenate(hots, axis=0), table, preferred_element_type=F32).astype(BF16)
    keys = jnp.dot(near, wk_ref[...], preferred_element_type=F32).astype(BF16)
    values = jnp.dot(near, wv_ref[...], preferred_element_type=F32).astype(BF16)
    far = jnp.dot(near, wdst_ref[...], preferred_element_type=F32).astype(BF16)
    query = jnp.dot(norm_ref[...], wq_ref[...], preferred_element_type=F32).astype(BF16).astype(F32)
    own = jnp.dot(norm_ref[...], wsrc_ref[...], preferred_element_type=F32)
    edges = edges_ref[...].reshape(768, 512)
    before = jnp.dot(edges, win_ref[...], preferred_element_type=F32)
    hidden = []
    for k in range(6):
        rows = slice(128 * k, 128 * k + 128)
        hidden.append(silu(before[rows] + own + far[rows].astype(F32)).astype(BF16))
    edge_sum = edges.astype(F32) + jnp.dot(jnp.concatenate(hidden, axis=0), wout_ref[...], preferred_element_type=F32)
    edge_out_ref[...] = edge_sum.astype(BF16).reshape(6, 128, 512)
    head = jnp.where(iota((8, 512), 0) == iota((8, 512), 1) // 64, 1.0, 0.0)
    scaled = (head * 0.125).astype(BF16)
    bhigh, blow = split(wbias_ref[...])
    mixer = jnp.concatenate([scaled, scaled, bhigh, bhigh, blow], axis=1)
    scores = []
    for k in range(6):
        rows = slice(128 * k, 128 * k + 128)
        qhigh, qlow = split(query * keys[rows].astype(F32))
        ehigh, elow = split(edge_sum[rows])
        score = contract_last(jnp.concatenate([qhigh, qlow, ehigh, elow, ehigh], axis=1), mixer)
        scores.append(jnp.where(info[:, 6:7] > k, score, -1e30))
    most = functools.reduce(jnp.maximum, scores)
    powers = [jnp.exp(score - most) for score in scores]
    total = functools.reduce(jnp.add, powers)
    attended = None
    for k in range(6):
        weight = (powers[k] / total).astype(BF16)
        spread = jnp.dot(weight, head.astype(BF16), preferred_element_type=F32)
        term = spread * values[128 * k : 128 * k + 128].astype(F32)
        attended = term if attended is None else attended + term
    middle = atm_ref[...] + jnp.dot(attended.astype(BF16), wo_ref[...], preferred_element_type=F32)
    normed2 = unit_norm(middle, gain_ref[...], 1e-5).astype(BF16)
    expanded = silu(jnp.dot(normed2, up_ref[...], preferred_element_type=F32)).astype(BF16)
    out_ref[...] = (middle + jnp.dot(expanded, down_ref[...], preferred_element_type=F32)).astype(BF16)
    for copy in copies:
        copy.wait()


def atmosphere(*args):
    return pl.pallas_call(
        atmosphere_kernel,
        out_shape=(jax.ShapeDtypeStruct((128, 512), BF16), jax.ShapeDtypeStruct((6, 128, 512), BF16))
        + tuple(jax.ShapeDtypeStruct(*item) for item in HALO),
        in_specs=[vmem()] * (len(args) - 2) + [anywhere()] * 2,
        out_specs=(vmem(), vmem()) + (anywhere(),) * 8,
        scratch_shapes=[pltpu.SemaphoreType.DMA((8,))] * 2,
        compiler_params=pltpu.CompilerParams(vmem_limit_bytes=60 << 20, collective_id=2, has_side_effects=True),
        name="atmosphere",
    )(*args)


def local(atm_state, edge_state, neighbours, degree, surface_fields, ocean_state, wet_mask, flux_columns, flux_weights,
          surface_columns, surface_weights, w_surface, w_flux, ln1_gain, w_query, w_key, w_value, w_out, w_edge_in, w_edge_src,
          w_edge_dst, w_edge_out, w_bias, ln2_gain, w_up, w_down, w_flux_in, dw_kernel, dw_bias, ocean_gain, w_expand, w_reduce,
          layer_scale):
    x, edge, atm_in, normed = front(
        w_flux.T, surface_fields.reshape(128, 128), flux_columns, flux_weights, ocean_state, wet_mask, w_flux_in, surface_columns,
        surface_weights, atm_state, w_surface, ln1_gain.reshape(1, 512))
    ocean = (dw_kernel.transpose(1, 0, 2), dw_bias, ocean_gain, layer_scale, w_expand, w_reduce, wet_mask)
    x, edge, rims = ocean_first(*ocean, x, edge, normed)
    atm_out, edge_out, *halo = atmosphere(
        normed, rims.reshape(512, 512), atm_in, edge_state.transpose(1, 0, 2), neighbours.T, degree.reshape(1, 128), w_query, w_key,
        w_value, w_out, w_edge_in, w_edge_src, w_edge_dst, w_edge_out, w_bias.T, ln2_gain.reshape(1, 512), w_up, w_down, x, edge)
    ocean_out = ocean_last(*ocean, x, *halo)
    return atm_out, edge_out.transpose(1, 0, 2), ocean_out


def solution(mesh):
    whole, rows = ("comp", "lat", "lon"), ("comp", "lat")
    in_specs = (
        P(whole, None), P(whole, None, None), P(whole, None), P(whole), P(None, rows, "lon"), P(rows, "lon", None), P(rows, "lon"),
        P(None, rows, "lon"), P(None, rows, "lon"), P(None, whole), P(None, whole)) + (P(),) * 22
    out_specs = (P(whole, None), P(whole, None, None), P(rows, "lon", None))
    return jax.shard_map(local, mesh=mesh, in_specs=in_specs, out_specs=out_specs, check_vma=False)
```

```python
import functools
import jax
import jax.numpy as jnp
from jax import lax
from jax.experimental import pallas as pl
from jax.experimental.pallas import tpu as pltpu
from jax.sharding import PartitionSpec as P

F32 = jnp.float32
BF16 = jnp.bfloat16


def iota(shape, axis):
    return lax.broadcasted_iota(jnp.int32, shape, axis)


def swap_blocks(parts):
    lane = iota(parts[0].shape, 1)
    upper = lane >= 64
    odd = (lane // 32) % 2 == 1
    first = []
    for low in range(2):
        a, b = parts[low], parts[low + 2]
        first.append((jnp.where(upper, pltpu.roll(b, 64, 1), a), jnp.where(upper, b, pltpu.roll(a, 64, 1))))
    out = [None] * 4
    for side in range(2):
        a, b = first[0][side], first[1][side]
        out[2 * side] = jnp.where(odd, pltpu.roll(b, 32, 1), a)
        out[2 * side + 1] = jnp.where(odd, b, pltpu.roll(a, 96, 1))
    return out


def order_matrix():
    row, col = iota((128, 128), 0), iota((128, 128), 1)
    return jnp.where(col == 8 * (row % 16) + row // 16, 1.0, 0.0)


def build_weights(block, kernel_ref, w_ref):
    eye = jnp.where(iota((32, 256), 0) == iota((32, 256), 1) % 32, 1.0, 0.0).astype(BF16)

    def body(tap, carry):
        rows = kernel_ref[pl.ds(tap * 7, 7), block]
        stack = jnp.concatenate([rows, jnp.zeros((17, 256), F32)], axis=0)
        shifted = [stack if j == 0 else pltpu.roll(stack, j, 0) for j in range(8)]
        for t in range(2):
            halves = []
            for h in range(2):
                halves.append(swap_blocks([shifted[4 * h + i][0:16, 128 * t : 128 * t + 128] for i in range(4)]))
            for u in range(4):
                line = jnp.concatenate([halves[0][u], halves[1][u]], axis=1)
                for n in range(16):
                    spread = jnp.broadcast_to(line[n : n + 1], (16, 256)).astype(BF16)
                    w_ref[4 * t + u, pl.ds(tap * 512 + n * 32, 32)] = eye * jnp.concatenate([spread, spread], axis=0)
        return carry

    lax.fori_loop(0, 7, body, 0)


def fill_rows(pad_ref, side_ref, xt_ref):
    source, target = iota((512, 512), 0), iota((512, 512), 1)
    moved = (source // 32 % 4) * 128 + (source // 128) * 32 + source % 32
    mixer = jnp.where(moved == target, 1.0, 0.0).astype(BF16)
    place = iota((608, 128), 0) % 16
    first, last, low = place == 0, place == 15, iota((608, 128), 1) < 96
    for t in range(2):
        lanes = slice(128 * t, 128 * t + 128)
        for h in range(2):
            tiles = [pad_ref[:, (p + 5) % 8, :, lanes].reshape(608, 128) for p in range(4 * h, 4 * h + 4)]
            mixed = jnp.dot(jnp.concatenate(tiles, axis=1), mixer, preferred_element_type=F32)
            edges = swap_blocks([side_ref[n, :, lanes] for n in ((0, 1, 2, 3) if h == 0 else (4, 5, 5, 5))])
            for u in range(4):
                part = mixed[:, 128 * u : 128 * u + 128]
                edge = jnp.broadcast_to(edges[u][0:38].reshape(38, 1, 128), (38, 16, 128)).reshape(608, 128)
                later = jnp.where(last, edge, pltpu.roll(part, 607, 0))
                if h == 0:
                    zero_view = jnp.where(low, jnp.where(first, edge, pltpu.roll(part, 1, 0)), part)
                    one_view = jnp.where(low, part, later)
                else:
                    zero_view, one_view = part, later
                for q, view in enumerate((zero_view, one_view)):
                    xt_ref[q, 4 * t + u, :, :, 128 * h : 128 * h + 128] = view.astype(BF16).reshape(38, 16, 128)


def block_body(last, kernel_ref, bias_ref, gain_ref, scale_ref, up_ref, down_ref, mask_ref, arrived, sides,
               out_ref, edge_ref, pad_ref, w_ref, xt_ref, conv_ref, stat_ref, rms_ref, side_ref, lines_ref):
    block = 1 if last else 0
    build_weights(block, kernel_ref, w_ref)
    arrived()
    west_ref, east_ref, nw_ref, ne_ref, sw_ref, se_ref = sides
    side_ref[0:3, 3:35] = west_ref[...].astype(F32)
    side_ref[3:6, 3:35] = east_ref[...].astype(F32)
    for at, north_ref, south_ref in ((0, nw_ref, sw_ref), (3, ne_ref, se_ref)):
        side_ref[at : at + 3, 0:3] = north_ref[...].astype(F32)[:, 13:16]
        side_ref[at : at + 3, 35:38] = south_ref[...].astype(F32)[:, 0:3]
    side_ref[:, 38:40] = jnp.zeros((6, 2, 256), F32)
    fill_rows(pad_ref, side_ref, xt_ref)

    grouped = []
    lines = jnp.concatenate([bias_ref[block : block + 1]] + [gain_ref[block : block + 1]] * 7, axis=0)
    scale = 0.5 * scale_ref[block : block + 1]
    for t in range(2):
        part = lines[:, 128 * t : 128 * t + 128]
        grouped += [jnp.concatenate([v, v], axis=1) for v in swap_blocks([part] * 4)]

    for g in range(8):
        pieces = []
        for a in range(7):
            for q in range(2):
                pieces.append(xt_ref[q, g, a : a + 32].reshape(512, 256))
        acc = jnp.dot(jnp.concatenate(pieces, axis=1), w_ref[g], preferred_element_type=F32) + grouped[g][0:1]
        conv_ref[g] = acc
        stat_ref[...] = acc if g == 0 else stat_ref[...] + acc

    same = jnp.where(iota((256, 256), 0) // 32 == iota((256, 256), 1) // 32, 1.0 / 256, 0.0).astype(BF16)
    same2 = jnp.concatenate([same, same], axis=0)

    def spread(values):
        high = values.astype(BF16)
        low = (values - high.astype(F32)).astype(BF16)
        return jnp.dot(jnp.concatenate([high, low], axis=1), same2, preferred_element_type=F32)

    stat_ref[...] = spread(stat_ref[...])

    def squares(n, carry):
        at = pl.ds(pl.multiple_of(n * 64, 64), 64)
        mean = stat_ref[at]
        total = None
        for g in range(8):
            centre = conv_ref[g, at] - mean
            total = centre * centre if total is None else total + centre * centre
        rms_ref[at] = total
        return carry

    lax.fori_loop(0, 8, squares, 0)
    rms_ref[...] = lax.rsqrt(spread(rms_ref[...]) + 1e-6)
    order = order_matrix()
    ones = jnp.ones((128, 256), BF16)
    order_back = jnp.where(iota((128, 128), 0) == 8 * (iota((128, 128), 1) % 16) + iota((128, 128), 1) // 16, 1.0, 0.0).astype(BF16)

    def mlp(n, carry):
        at = pl.ds(pl.multiple_of(n * 64, 64), 64)
        mean, rms = stat_ref[at], rms_ref[at]
        norm = [((conv_ref[g, at] - mean) * rms * grouped[g][1:2]).astype(BF16) for g in range(8)]
        tiles = [[None] * 2 for _ in range(8)]
        for h in range(2):
            for t in range(2):
                done = swap_blocks([norm[4 * t + u][:, 128 * h : 128 * h + 128] for u in range(4)])
                for i in range(4):
                    tiles[4 * h + i][t] = done[i]
        full = [jnp.concatenate(pair, axis=1) for pair in tiles]
        rows = jnp.concatenate([full[j][16 * k : 16 * k + 16] for k in range(4) for j in range(8)], axis=0)
        wide = jnp.dot(rows, up_ref[block], preferred_element_type=F32)
        wide = wide.astype(BF16)
        grown = wide + wide * jnp.tanh(wide * (0.7978845608028654 + 0.035677408136300125 * wide * wide))
        small = jnp.dot(grown, down_ref[block], preferred_element_type=F32)
        picks = jnp.concatenate([order * mask_ref[pl.ds(4 * n + k, 1)].astype(F32) for k in range(4)], axis=0).astype(BF16)
        sea = jnp.dot(picks, ones, preferred_element_type=F32)
        base = pad_ref[pl.ds(3 + 4 * n, 4)].reshape(512, 256).astype(F32)
        fresh = sea * (base + scale * small)
        fresh16 = fresh.astype(BF16)
        if last:
            for k in range(4):
                natural = jnp.dot(order_back, fresh16[128 * k : 128 * k + 128], preferred_element_type=F32)
                out_ref[4 * n + k] = natural.astype(BF16)
        else:
            out_ref[pl.ds(4 * n, 4)] = fresh16.reshape(4, 8, 16, 256)
            for k in range(4):
                keep_edges(lines_ref, 4 * n + k, fresh[128 * k : 128 * k + 128], (0, 16, 32, 95, 111, 127))
        return carry

    lax.fori_loop(0, 8, mlp, 0, unroll=4)
    if not last:
        edge_ref[...] = lines_ref[...].astype(BF16)


def keep_edges(lines_ref, r, rows, at):
    for n, p in enumerate(at):
        lines_ref[n, pl.ds(r, 1)] = rows[p : p + 1]


def vmem():
    return pl.BlockSpec(memory_space=pltpu.VMEM)


def anywhere():
    return pl.BlockSpec(memory_space=pl.ANY)


def split(values):
    high = values.astype(BF16)
    return high, (values - high.astype(F32)).astype(BF16)


def contract_last(a, b):
    return lax.dot_general(a, b, (((1,), (1,)), ((), ())), preferred_element_type=F32)


def contract_first(a, b):
    return lax.dot_general(a, b, (((0,), (0,)), ((), ())), preferred_element_type=F32)


def unit_norm(values, gain, epsilon):
    centre = values - jnp.mean(values, axis=-1, keepdims=True)
    spread = jnp.mean(centre * centre, axis=-1, keepdims=True)
    return centre * lax.rsqrt(spread + epsilon) * gain


AROUND = [(dr, dc) for dr in (-1, 0, 1) for dc in (-1, 0, 1) if (dr, dc) != (0, 0)]
ROWS = [((3, 8, 16, 256), BF16)] * 2
SIDES = [((3, 32, 256), BF16)] * 2 + [((3, 16, 256), BF16)] * 4
BLOCK_SCRATCH = [
    ((38, 8, 16, 256), BF16),
    ((8, 3584, 256), BF16), ((2, 8, 38, 16, 256), BF16), ((8, 512, 256), F32), ((512, 256), F32), ((512, 256), F32),
    ((6, 40, 256), F32), ((6, 32, 256), F32)]


def greet(devices):
    barrier = pltpu.get_barrier_semaphore()
    for device in devices:
        pl.semaphore_signal(barrier, inc=1, device_id=device, device_id_type=pl.DeviceIdType.MESH)
    pl.semaphore_wait(barrier, len(devices))


def neighbour(dr, dc):
    band = lax.axis_index("comp") * 8 + lax.axis_index("lat")
    row = lax.rem(band + 16 + dr, 16)
    return {"comp": row // 8, "lat": lax.rem(row, 8), "lon": lax.rem(lax.axis_index("lon") + 16 + dc, 16)}


def send(source, target, send_sem, recv_sem, device):
    copy = pltpu.make_async_remote_copy(
        src_ref=source, dst_ref=target, send_sem=send_sem, recv_sem=recv_sem, device_id=device, device_id_type=pl.DeviceIdType.MESH)
    copy.start()
    return copy


def start_halo(x_ref, edge_ref, halo, send_sem, recv_sem):
    north, south, west, east, nw, ne, sw, se = halo
    left, right = edge_ref.at[pl.ds(0, 3)], edge_ref.at[pl.ds(3, 3)]
    top, bottom = pl.ds(0, 16), pl.ds(16, 16)
    moves = [
        (x_ref.at[pl.ds(0, 3)], south, -1, 0), (x_ref.at[pl.ds(29, 3)], north, 1, 0), (left, east, 0, -1), (right, west, 0, 1),
        (edge_ref.at[pl.ds(0, 3), top], se, -1, -1), (edge_ref.at[pl.ds(3, 3), top], sw, -1, 1),
        (edge_ref.at[pl.ds(0, 3), bottom], ne, 1, -1), (edge_ref.at[pl.ds(3, 3), bottom], nw, 1, 1)]
    return [
        send(source, target, send_sem.at[n], recv_sem.at[n], neighbour(dr, dc))
        for n, (source, target, dr, dc) in enumerate(moves)]


def first_kernel(*refs):
    ins, x_ref, edge_ref, norm_ref = refs[:7], refs[7], refs[8], refs[9]
    out_ref, line_ref, rims_ref = refs[10:13]
    scratch, sides = refs[13:21], refs[21:27]
    send_sem, recv_sem, local_sem = refs[27:30]
    pad_ref = scratch[0]
    own = pltpu.make_async_copy(x_ref, pad_ref.at[pl.ds(3, 32)], local_sem)
    own.start()
    greet([neighbour(dr, dc) for dr, dc in AROUND])
    copies = start_halo(x_ref, edge_ref, (pad_ref.at[pl.ds(0, 3)], pad_ref.at[pl.ds(35, 3)]) + tuple(sides), send_sem, recv_sem)
    rims = []

    def arrived():
        own.wait()
        for copy in copies:
            copy.wait()
        for n, (dr, dc) in enumerate(AROUND):
            slot = (1 - dr) * 3 + 1 - dc
            slot = slot - 1 if slot > 4 else slot
            rims.append(send(norm_ref.at[pl.ds(0, 64)], rims_ref.at[slot], send_sem.at[8 + n], recv_sem.at[8 + n], neighbour(dr, dc)))

    block_body(False, *ins, arrived, sides, out_ref, line_ref, *scratch)
    for copy in rims:
        copy.wait()


def ocean_first(*args):
    scratch = [pltpu.VMEM(*item) for item in BLOCK_SCRATCH + SIDES] + [pltpu.SemaphoreType.DMA((16,))] * 2 + [pltpu.SemaphoreType.DMA]
    return pl.pallas_call(
        first_kernel,
        out_shape=(
            jax.ShapeDtypeStruct((32, 8, 16, 256), BF16), jax.ShapeDtypeStruct((6, 32, 256), BF16),
            jax.ShapeDtypeStruct((8, 64, 512), BF16)),
        in_specs=[vmem()] * 7 + [anywhere(), vmem(), vmem()],
        out_specs=(vmem(), vmem(), anywhere()),
        scratch_shapes=scratch,
        compiler_params=pltpu.CompilerParams(vmem_limit_bytes=60 << 20, collective_id=1, has_side_effects=True),
        name="ocean_first",
    )(*args)


def last_kernel(*refs):
    ins, x_ref, north_ref, south_ref, sides = refs[:7], refs[7], refs[8], refs[9], refs[10:16]
    out_ref, scratch, sems = refs[16], refs[17:25], refs[25]
    pad_ref = scratch[0]
    copies = [
        pltpu.make_async_copy(x_ref, pad_ref.at[pl.ds(3, 32)], sems.at[0]),
        pltpu.make_async_copy(north_ref, pad_ref.at[pl.ds(0, 3)], sems.at[1]),
        pltpu.make_async_copy(south_ref, pad_ref.at[pl.ds(35, 3)], sems.at[2])]
    for copy in copies:
        copy.start()

    def arrived():
        for copy in copies:
            copy.wait()

    block_body(True, *ins, arrived, sides, out_ref, None, *scratch)


def ocean_last(*args):
    return pl.pallas_call(
        last_kernel,
        out_shape=jax.ShapeDtypeStruct((32, 128, 256), BF16),
        in_specs=[vmem()] * 7 + [anywhere()] * 3 + [vmem()] * 6,
        out_specs=vmem(),
        scratch_shapes=[pltpu.VMEM(*item) for item in BLOCK_SCRATCH] + [pltpu.SemaphoreType.DMA((3,))],
        compiler_params=pltpu.CompilerParams(vmem_limit_bytes=60 << 20),
        name="ocean_last",
    )(*args)


def front_kernel(wflux_ref, fields_ref, cols_ref, fluxw_ref, ocean_ref, mask_ref, wfin_ref, scols_ref, sw_ref, state_ref, wsurf_ref,
                 gain_ref, x_ref, edge_ref, atm_ref, norm_ref, flux_own, field_own, flux_tab, field_tab, lines_ref,
                 flux_send, flux_recv, field_send, field_recv, pass_send, pass_recv):
    me = lax.axis_index("lon")
    side, deep = me // 8, lax.rem(me, 8)
    partner = {"lon": lax.rem(me + 8, 16)}
    high, low = split(wflux_ref[...])
    both = contract_last(jnp.concatenate([high, low], axis=0), state_ref[...])
    fluxes = jnp.concatenate([both[0:4] + both[4:8], jnp.zeros((12, 128), F32)], axis=0).astype(BF16)
    fields = fields_ref[...].astype(BF16)
    flux_own[...] = fluxes
    field_own[...] = fields
    flux_tab[me] = fluxes
    field_tab[me] = fields
    greet([{"lon": lax.rem(me + step, 16)} for step in range(1, 16)])
    small_copies = [
        send(flux_own, flux_tab.at[me], flux_send.at[step], flux_recv.at[step], {"lon": lax.rem(me + step, 16)})
        for step in range(1, 16)]
    field_copies = [
        send(field_own, field_tab.at[me], field_send.at[step], field_recv.at[step], {"lon": side * 8 + lax.rem(deep + step, 8)})
        for step in range(1, 8)]
    pass_copies = [send(field_own, field_tab.at[me], pass_send.at[0], pass_recv.at[0], partner)]
    for copy in small_copies:
        copy.wait()

    pairs = []
    for p in range(8):
        pairs.append(jnp.concatenate([flux_tab[2 * p, 0:4], flux_tab[2 * p + 1, 0:4]], axis=0))
    small = jnp.concatenate(pairs, axis=0)
    node = iota((128, 128), 0)
    half = iota((8, 128), 0) // 4
    wide = jnp.concatenate([wfin_ref[...], wfin_ref[...]], axis=0)
    whigh, wlow = split(wide)
    zero8 = jnp.zeros((8, 256), BF16)
    right = jnp.concatenate([
        jnp.concatenate([whigh, zero8], axis=1), jnp.concatenate([whigh, zero8], axis=1),
        jnp.concatenate([wlow, zero8], axis=1), jnp.concatenate([zero8, jnp.ones((8, 256), BF16)], axis=1)], axis=0)
    order = order_matrix().astype(BF16)
    top_row = iota((8, 128), 0) == 0

    def row(r, carry):
        ids = [cols_ref[k, pl.ds(r, 1)] for k in range(4)]
        hots = [jnp.where(node == (i & 127), 1.0, 0.0).astype(BF16) for i in ids]
        picked = jnp.dot(small, jnp.concatenate(hots, axis=1), preferred_element_type=F32)
        cell = None
        for k in range(4):
            part = (ids[k] >> 7) & 15
            level = part >> 1
            total = None
            for p in range(8):
                term = jnp.where(level == p, picked[8 * p : 8 * p + 8, 128 * k : 128 * k + 128], 0.0)
                total = term if total is None else total + term
            total = jnp.where(half == (part & 1), total, 0.0) * fluxw_ref[k, pl.ds(r, 1)]
            cell = total if cell is None else cell + total
        high, low = split(cell)
        sea = jnp.where(top_row, mask_ref[pl.ds(r, 1)].astype(F32), 0.0).astype(BF16)
        both = contract_first(jnp.concatenate([high, low, high, sea], axis=0), right)
        fresh = both[:, 256:512] * (ocean_ref[r].astype(F32) + both[:, 0:256])
        fresh16 = fresh.astype(BF16)
        x_ref[r] = jnp.dot(order, fresh16, preferred_element_type=F32).astype(BF16).reshape(8, 16, 256)
        keep_edges(lines_ref, r, fresh, (0, 1, 2, 125, 126, 127))
        return carry

    lax.fori_loop(0, 16, row, 0, unroll=8)
    for step in range(1, 8):
        field_copies[step - 1].wait()
        block = field_tab.at[side * 8 + lax.rem(deep + 8 - step, 8)]
        pass_copies.append(send(block, block, pass_send.at[step], pass_recv.at[step], partner))
    lax.fori_loop(16, 32, row, 0, unroll=8)
    edge_ref[...] = lines_ref[...].astype(BF16)
    for copy in pass_copies:
        copy.wait()

    ids = jnp.concatenate([scols_ref[k : k + 1] for k in range(4)], axis=1)
    cell = ids & 2047
    level = (ids >> 11) & 31
    spot = iota((128, 512), 0)
    hots, tabs = [], []
    for p in range(16):
        hots.append(jnp.where(spot + 128 * p == cell, 1.0, 0.0).astype(BF16))
        tabs.append(field_tab[p])
    picked = jnp.dot(jnp.concatenate(tabs, axis=1), jnp.concatenate(hots, axis=0), preferred_element_type=F32)
    weight = jnp.concatenate([sw_ref[k : k + 1] for k in range(4)], axis=1)
    chosen = jnp.where(iota((32, 512), 0) == level, weight, 0.0)
    sums = []
    for s in range(4):
        term = jnp.sum(picked[32 * s : 32 * s + 32] * chosen, axis=0, keepdims=True)
        sums.append(term[:, 0:128] + term[:, 128:256] + term[:, 256:384] + term[:, 384:512])
    nodes = jnp.concatenate(sums + [jnp.zeros((4, 128), F32)], axis=0)
    high, low = split(nodes)
    whigh, wlow = split(jnp.concatenate([wsurf_ref[...], jnp.zeros((4, 512), F32)], axis=0))
    zeros = jnp.zeros((8, 128), BF16)
    lift = contract_first(jnp.concatenate([high, low, high, zeros], axis=0), jnp.concatenate([whigh, whigh, wlow, jnp.zeros((8, 512), BF16)], axis=0))
    atm_in = state_ref[...].astype(F32) + lift
    atm_ref[...] = atm_in
    norm_ref[...] = unit_norm(atm_in, gain_ref[...], 1e-5).astype(BF16)


def front(*args):
    return pl.pallas_call(
        front_kernel,
        out_shape=(
            jax.ShapeDtypeStruct((32, 8, 16, 256), BF16),
            jax.ShapeDtypeStruct((6, 32, 256), BF16),
            jax.ShapeDtypeStruct((128, 512), F32),
            jax.ShapeDtypeStruct((128, 512), BF16),
        ),
        in_specs=[vmem()] * len(args),
        out_specs=tuple([vmem()] * 4),
        scratch_shapes=[
            pltpu.VMEM((16, 128), BF16), pltpu.VMEM((128, 128), BF16), pltpu.VMEM((16, 16, 128), BF16), pltpu.VMEM((16, 128, 128), BF16),
            pltpu.VMEM((6, 32, 256), F32)] + [pltpu.SemaphoreType.DMA((16,))] * 2 + [pltpu.SemaphoreType.DMA((8,))] * 4,
        compiler_params=pltpu.CompilerParams(vmem_limit_bytes=60 << 20, collective_id=0, has_side_effects=True),
        name="front",
    )(*args)


def silu(values):
    return values * jax.nn.sigmoid(values)


def atmosphere_kernel(norm_ref, rims_ref, atm_ref, edges_ref, near_ref, degree_ref, wq_ref, wk_ref, wv_ref, wo_ref, win_ref, wsrc_ref,
                      wdst_ref, wout_ref, wbias_ref, gain_ref, up_ref, down_ref, x_ref, line_ref, out_ref, edge_out_ref, *rest):
    greet([neighbour(dr, dc) for dr, dc in AROUND])
    copies = start_halo(x_ref, line_ref, rest[:8], rest[8], rest[9])
    band = lax.axis_index("comp") * 8 + lax.axis_index("lat")
    col = lax.axis_index("lon")
    ids = near_ref[...]
    part, inside = ids >> 7, ids & 127
    down = (part >> 4) - band
    right = (((part & 15) - col + 1) & 15) - 1
    spot = (down + 1) * 3 + right + 1
    spot = spot - jnp.where(spot > 4, 1, 0)
    at = jnp.where((down == 0) & (right == 0), inside, 128 + spot * 64 + inside)
    info = jnp.concatenate([at, degree_ref[...], degree_ref[...]], axis=0).astype(F32)
    info = info.T
    table = jnp.concatenate([norm_ref[...], rims_ref[...]], axis=0)
    lane = iota((128, 640), 1).astype(F32)
    hots = [jnp.where(lane == info[:, k : k + 1], 1.0, 0.0).astype(BF16) for k in range(6)]
    near = jnp.dot(jnp.concatenate(hots, axis=0), table, preferred_element_type=F32).astype(BF16)
    keys = jnp.dot(near, wk_ref[...], preferred_element_type=F32).astype(BF16)
    values = jnp.dot(near, wv_ref[...], preferred_element_type=F32).astype(BF16)
    far = jnp.dot(near, wdst_ref[...], preferred_element_type=F32).astype(BF16)
    query = jnp.dot(norm_ref[...], wq_ref[...], preferred_element_type=F32).astype(BF16).astype(F32)
    own = jnp.dot(norm_ref[...], wsrc_ref[...], preferred_element_type=F32)
    edges = edges_ref[...].reshape(768, 512)
    before = jnp.dot(edges, win_ref[...], preferred_element_type=F32)
    hidden = []
    for k in range(6):
        rows = slice(128 * k, 128 * k + 128)
        hidden.append(silu(before[rows] + own + far[rows].astype(F32)).astype(BF16))
    edge_sum = edges.astype(F32) + jnp.dot(jnp.concatenate(hidden, axis=0), wout_ref[...], preferred_element_type=F32)
    edge_out_ref[...] = edge_sum.astype(BF16).reshape(6, 128, 512)
    head = jnp.where(iota((8, 512), 0) == iota((8, 512), 1) // 64, 1.0, 0.0)
    scaled = (head * 0.125).astype(BF16)
    bhigh, blow = split(wbias_ref[...])
    mixer = jnp.concatenate([scaled, scaled, bhigh, bhigh, blow], axis=1)
    scores = []
    for k in range(6):
        rows = slice(128 * k, 128 * k + 128)
        qhigh, qlow = split(query * keys[rows].astype(F32))
        ehigh, elow = split(edge_sum[rows])
        score = contract_last(jnp.concatenate([qhigh, qlow, ehigh, elow, ehigh], axis=1), mixer)
        scores.append(jnp.where(info[:, 6:7] > k, score, -1e30))
    most = functools.reduce(jnp.maximum, scores)
    powers = [jnp.exp(score - most) for score in scores]
    total = functools.reduce(jnp.add, powers)
    attended = None
    for k in range(6):
        weight = (powers[k] / total).astype(BF16)
        spread = jnp.dot(weight, head.astype(BF16), preferred_element_type=F32)
        term = spread * values[128 * k : 128 * k + 128].astype(F32)
        attended = term if attended is None else attended + term
    middle = atm_ref[...] + jnp.dot(attended.astype(BF16), wo_ref[...], preferred_element_type=F32)
    normed2 = unit_norm(middle, gain_ref[...], 1e-5).astype(BF16)
    expanded = silu(jnp.dot(normed2, up_ref[...], preferred_element_type=F32)).astype(BF16)
    out_ref[...] = (middle + jnp.dot(expanded, down_ref[...], preferred_element_type=F32)).astype(BF16)
    for copy in copies:
        copy.wait()


def atmosphere(*args):
    return pl.pallas_call(
        atmosphere_kernel,
        out_shape=(jax.ShapeDtypeStruct((128, 512), BF16), jax.ShapeDtypeStruct((6, 128, 512), BF16))
        + tuple(jax.ShapeDtypeStruct(*item) for item in ROWS + SIDES),
        in_specs=[vmem()] * (len(args) - 2) + [anywhere()] * 2,
        out_specs=(vmem(), vmem()) + (anywhere(),) * 8,
        scratch_shapes=[pltpu.SemaphoreType.DMA((8,))] * 2,
        compiler_params=pltpu.CompilerParams(vmem_limit_bytes=60 << 20, collective_id=2, has_side_effects=True),
        name="atmosphere",
    )(*args)


def local(atm_state, edge_state, neighbours, degree, surface_fields, ocean_state, wet_mask, flux_columns, flux_weights,
          surface_columns, surface_weights, w_surface, w_flux, ln1_gain, w_query, w_key, w_value, w_out, w_edge_in, w_edge_src,
          w_edge_dst, w_edge_out, w_bias, ln2_gain, w_up, w_down, w_flux_in, dw_kernel, dw_bias, ocean_gain, w_expand, w_reduce,
          layer_scale):
    x, edge, atm_in, normed = front(
        w_flux.T, surface_fields.reshape(128, 128), flux_columns, flux_weights, ocean_state, wet_mask, w_flux_in, surface_columns,
        surface_weights, atm_state, w_surface, ln1_gain.reshape(1, 512))
    ocean = (dw_kernel.transpose(1, 0, 2), dw_bias, ocean_gain, layer_scale, w_expand, w_reduce, wet_mask)
    x, edge, rims = ocean_first(*ocean, x, edge, normed)
    atm_out, edge_out, *halo = atmosphere(
        normed, rims.reshape(512, 512), atm_in, edge_state.transpose(1, 0, 2), neighbours.T, degree.reshape(1, 128), w_query, w_key,
        w_value, w_out, w_edge_in, w_edge_src, w_edge_dst, w_edge_out, w_bias.T, ln2_gain.reshape(1, 512), w_up, w_down, x, edge)
    ocean_out = ocean_last(*ocean, x, *halo)
    return atm_out, edge_out.transpose(1, 0, 2), ocean_out


def solution(mesh):
    whole, rows = ("comp", "lat", "lon"), ("comp", "lat")
    in_specs = (
        P(whole, None), P(whole, None, None), P(whole, None), P(whole), P(None, rows, "lon"), P(rows, "lon", None), P(rows, "lon"),
        P(None, rows, "lon"), P(None, rows, "lon"), P(None, whole), P(None, whole)) + (P(),) * 22
    out_specs = (P(whole, None), P(whole, None, None), P(rows, "lon", None))
    return jax.shard_map(local, mesh=mesh, in_specs=in_specs, out_specs=out_specs, check_vma=False)
```

```python
import functools
import jax
import jax.numpy as jnp
from jax import lax
from jax.experimental import pallas as pl
from jax.experimental.pallas import tpu as pltpu
from jax.sharding import PartitionSpec as P

F32 = jnp.float32
BF16 = jnp.bfloat16


def iota(shape, axis):
    return lax.broadcasted_iota(jnp.int32, shape, axis)


def swap_blocks(parts):
    lane = iota(parts[0].shape, 1)
    upper = lane >= 64
    odd = (lane // 32) % 2 == 1
    first = []
    for low in range(2):
        a, b = parts[low], parts[low + 2]
        first.append((jnp.where(upper, pltpu.roll(b, 64, 1), a), jnp.where(upper, b, pltpu.roll(a, 64, 1))))
    out = [None] * 4
    for side in range(2):
        a, b = first[0][side], first[1][side]
        out[2 * side] = jnp.where(odd, pltpu.roll(b, 32, 1), a)
        out[2 * side + 1] = jnp.where(odd, b, pltpu.roll(a, 96, 1))
    return out


def order_matrix():
    row, col = iota((128, 128), 0), iota((128, 128), 1)
    return jnp.where(col == 8 * (row % 16) + row // 16, 1.0, 0.0)


def build_weights(block, kernel_ref, w_ref):
    eye = jnp.where(iota((32, 256), 0) == iota((32, 256), 1) % 32, 1.0, 0.0).astype(BF16)

    def body(tap, carry):
        rows = kernel_ref[pl.ds(tap * 7, 7), block]
        stack = jnp.concatenate([rows, jnp.zeros((17, 256), F32)], axis=0)
        shifted = [stack if j == 0 else pltpu.roll(stack, j, 0) for j in range(8)]
        for t in range(2):
            halves = []
            for h in range(2):
                halves.append(swap_blocks([shifted[4 * h + i][0:16, 128 * t : 128 * t + 128] for i in range(4)]))
            for u in range(4):
                line = jnp.concatenate([halves[0][u], halves[1][u]], axis=1)
                for n in range(16):
                    spread = jnp.broadcast_to(line[n : n + 1], (16, 256)).astype(BF16)
                    w_ref[4 * t + u, pl.ds(tap * 512 + n * 32, 32)] = eye * jnp.concatenate([spread, spread], axis=0)
        return carry

    lax.fori_loop(0, 7, body, 0)


def fill_rows(pad_ref, side_ref, xt_ref):
    source, target = iota((512, 512), 0), iota((512, 512), 1)
    moved = (source // 32 % 4) * 128 + (source // 128) * 32 + source % 32
    mixer = jnp.where(moved == target, 1.0, 0.0).astype(BF16)
    place = iota((608, 128), 0) % 16
    first, last, low = place == 0, place == 15, iota((608, 128), 1) < 96
    for t in range(2):
        lanes = slice(128 * t, 128 * t + 128)
        for h in range(2):
            tiles = [pad_ref[:, (p + 5) % 8, :, lanes].reshape(608, 128) for p in range(4 * h, 4 * h + 4)]
            mixed = jnp.dot(jnp.concatenate(tiles, axis=1), mixer, preferred_element_type=F32)
            edges = swap_blocks([side_ref[n, :, lanes] for n in ((0, 1, 2, 3) if h == 0 else (4, 5, 5, 5))])
            for u in range(4):
                part = mixed[:, 128 * u : 128 * u + 128]
                edge = jnp.broadcast_to(edges[u][0:38].reshape(38, 1, 128), (38, 16, 128)).reshape(608, 128)
                later = jnp.where(last, edge, pltpu.roll(part, 607, 0))
                if h == 0:
                    zero_view = jnp.where(low, jnp.where(first, edge, pltpu.roll(part, 1, 0)), part)
                    one_view = jnp.where(low, part, later)
                else:
                    zero_view, one_view = part, later
                for q, view in enumerate((zero_view, one_view)):
                    xt_ref[q, 4 * t + u, :, :, 128 * h : 128 * h + 128] = view.astype(BF16).reshape(38, 16, 128)


def block_body(last, kernel_ref, bias_ref, gain_ref, scale_ref, up_ref, down_ref, mask_ref, arrived, landed, sides,
               out_ref, edge_ref, pad_ref, w_ref, xt_ref, conv_ref, stat_ref, rms_ref, side_ref, lines_ref):
    block = 1 if last else 0
    build_weights(block, kernel_ref, w_ref)
    arrived()
    west_ref, east_ref, nw_ref, ne_ref, sw_ref, se_ref = sides
    side_ref[0:3, 3:35] = west_ref[...].astype(F32)
    side_ref[3:6, 3:35] = east_ref[...].astype(F32)
    for at, north_ref, south_ref in ((0, nw_ref, sw_ref), (3, ne_ref, se_ref)):
        side_ref[at : at + 3, 0:3] = north_ref[...].astype(F32)[:, 13:16]
        side_ref[at : at + 3, 35:38] = south_ref[...].astype(F32)[:, 0:3]
    side_ref[:, 38:40] = jnp.zeros((6, 2, 256), F32)
    fill_rows(pad_ref, side_ref, xt_ref)

    grouped = []
    lines = jnp.concatenate([bias_ref[block : block + 1]] + [gain_ref[block : block + 1]] * 7, axis=0)
    scale = 0.5 * scale_ref[block : block + 1]
    for t in range(2):
        part = lines[:, 128 * t : 128 * t + 128]
        grouped += [jnp.concatenate([v, v], axis=1) for v in swap_blocks([part] * 4)]

    for g in range(8):
        pieces = []
        for a in range(7):
            for q in range(2):
                pieces.append(xt_ref[q, g, a : a + 32].reshape(512, 256))
        acc = jnp.dot(jnp.concatenate(pieces, axis=1), w_ref[g], preferred_element_type=F32) + grouped[g][0:1]
        conv_ref[g] = acc
        stat_ref[...] = acc if g == 0 else stat_ref[...] + acc

    same = jnp.where(iota((256, 256), 0) // 32 == iota((256, 256), 1) // 32, 1.0 / 256, 0.0).astype(BF16)
    same2 = jnp.concatenate([same, same], axis=0)

    def spread(values):
        high = values.astype(BF16)
        low = (values - high.astype(F32)).astype(BF16)
        return jnp.dot(jnp.concatenate([high, low], axis=1), same2, preferred_element_type=F32)

    stat_ref[...] = spread(stat_ref[...])

    def squares(n, carry):
        at = pl.ds(pl.multiple_of(n * 64, 64), 64)
        mean = stat_ref[at]
        total = None
        for g in range(8):
            centre = conv_ref[g, at] - mean
            total = centre * centre if total is None else total + centre * centre
        rms_ref[at] = total
        return carry

    lax.fori_loop(0, 8, squares, 0)
    rms_ref[...] = lax.rsqrt(spread(rms_ref[...]) + 1e-6)
    order = order_matrix()
    ones = jnp.ones((128, 256), BF16)
    order_back = jnp.where(iota((128, 128), 0) == 8 * (iota((128, 128), 1) % 16) + iota((128, 128), 1) // 16, 1.0, 0.0).astype(BF16)

    def mlp(n, carry):
        at = pl.ds(pl.multiple_of(n * 64, 64), 64)
        mean, rms = stat_ref[at], rms_ref[at]
        norm = [((conv_ref[g, at] - mean) * rms * grouped[g][1:2]).astype(BF16) for g in range(8)]
        tiles = [[None] * 2 for _ in range(8)]
        for h in range(2):
            for t in range(2):
                done = swap_blocks([norm[4 * t + u][:, 128 * h : 128 * h + 128] for u in range(4)])
                for i in range(4):
                    tiles[4 * h + i][t] = done[i]
        full = [jnp.concatenate(pair, axis=1) for pair in tiles]
        rows = jnp.concatenate([full[j][16 * k : 16 * k + 16] for k in range(4) for j in range(8)], axis=0)
        wide = jnp.dot(rows, up_ref[...], preferred_element_type=F32)
        wide = wide.astype(BF16)
        grown = wide + wide * jnp.tanh(wide * (0.7978845608028654 + 0.035677408136300125 * wide * wide))
        small = jnp.dot(grown, down_ref[...], preferred_element_type=F32)
        picks = jnp.concatenate([order * mask_ref[pl.ds(4 * n + k, 1)].astype(F32) for k in range(4)], axis=0).astype(BF16)
        sea = jnp.dot(picks, ones, preferred_element_type=F32)
        base = pad_ref[pl.ds(3 + 4 * n, 4)].reshape(512, 256).astype(F32)
        fresh = sea * (base + scale * small)
        fresh16 = fresh.astype(BF16)
        if last:
            for k in range(4):
                natural = jnp.dot(order_back, fresh16[128 * k : 128 * k + 128], preferred_element_type=F32)
                out_ref[4 * n + k] = natural.astype(BF16)
        else:
            out_ref[pl.ds(4 * n, 4)] = fresh16.reshape(4, 8, 16, 256)
            for k in range(4):
                keep_edges(lines_ref, 4 * n + k, fresh[128 * k : 128 * k + 128], (0, 16, 32, 95, 111, 127))
        return carry

    landed()
    lax.fori_loop(0, 8, mlp, 0, unroll=4)
    if not last:
        edge_ref[...] = lines_ref[...].astype(BF16)


def keep_edges(lines_ref, r, rows, at):
    for n, p in enumerate(at):
        lines_ref[n, pl.ds(r, 1)] = rows[p : p + 1]


def vmem():
    return pl.BlockSpec(memory_space=pltpu.VMEM)


def anywhere():
    return pl.BlockSpec(memory_space=pl.ANY)


def split(values):
    high = values.astype(BF16)
    return high, (values - high.astype(F32)).astype(BF16)


def contract_last(a, b):
    return lax.dot_general(a, b, (((1,), (1,)), ((), ())), preferred_element_type=F32)


def contract_first(a, b):
    return lax.dot_general(a, b, (((0,), (0,)), ((), ())), preferred_element_type=F32)


def unit_norm(values, gain, epsilon):
    centre = values - jnp.mean(values, axis=-1, keepdims=True)
    spread = jnp.mean(centre * centre, axis=-1, keepdims=True)
    return centre * lax.rsqrt(spread + epsilon) * gain


AROUND = [(dr, dc) for dr in (-1, 0, 1) for dc in (-1, 0, 1) if (dr, dc) != (0, 0)]
ROWS = [((3, 8, 16, 256), BF16)] * 2
SIDES = [((3, 32, 256), BF16)] * 2 + [((3, 16, 256), BF16)] * 4
BLOCK_SCRATCH = [
    ((38, 8, 16, 256), BF16),
    ((8, 3584, 256), BF16), ((2, 8, 38, 16, 256), BF16), ((8, 512, 256), F32), ((512, 256), F32), ((512, 256), F32),
    ((6, 40, 256), F32), ((6, 32, 256), F32)]


WEIGHT_SCRATCH = [pltpu.VMEM((256, 1024), BF16), pltpu.VMEM((1024, 256), BF16), pltpu.SemaphoreType.DMA((2,))]


def greet(devices):
    barrier = pltpu.get_barrier_semaphore()
    for device in devices:
        pl.semaphore_signal(barrier, inc=1, device_id=device, device_id_type=pl.DeviceIdType.MESH)
    pl.semaphore_wait(barrier, len(devices))


def fetch(sources, targets, sems):
    copies = [pltpu.make_async_copy(source, target, sems.at[n]) for n, (source, target) in enumerate(zip(sources, targets))]
    for copy in copies:
        copy.start()

    def landed():
        for copy in copies:
            copy.wait()

    return landed


def neighbour(dr, dc):
    band = lax.axis_index("comp") * 8 + lax.axis_index("lat")
    row = lax.rem(band + 16 + dr, 16)
    return {"comp": row // 8, "lat": lax.rem(row, 8), "lon": lax.rem(lax.axis_index("lon") + 16 + dc, 16)}


def send(source, target, send_sem, recv_sem, device):
    copy = pltpu.make_async_remote_copy(
        src_ref=source, dst_ref=target, send_sem=send_sem, recv_sem=recv_sem, device_id=device, device_id_type=pl.DeviceIdType.MESH)
    copy.start()
    return copy


def start_halo(x_ref, edge_ref, halo, send_sem, recv_sem):
    north, south, west, east, nw, ne, sw, se = halo
    left, right = edge_ref.at[pl.ds(0, 3)], edge_ref.at[pl.ds(3, 3)]
    top, bottom = pl.ds(0, 16), pl.ds(16, 16)
    moves = [
        (x_ref.at[pl.ds(0, 3)], south, -1, 0), (x_ref.at[pl.ds(29, 3)], north, 1, 0), (left, east, 0, -1), (right, west, 0, 1),
        (edge_ref.at[pl.ds(0, 3), top], se, -1, -1), (edge_ref.at[pl.ds(3, 3), top], sw, -1, 1),
        (edge_ref.at[pl.ds(0, 3), bottom], ne, 1, -1), (edge_ref.at[pl.ds(3, 3), bottom], nw, 1, 1)]
    return [
        send(source, target, send_sem.at[n], recv_sem.at[n], neighbour(dr, dc))
        for n, (source, target, dr, dc) in enumerate(moves)]


def first_kernel(*refs):
    ins, x_ref, edge_ref, norm_ref = refs[:7], refs[7], refs[8], refs[9]
    out_ref, line_ref, rims_ref = refs[10:13]
    scratch, sides = refs[13:21], refs[21:27]
    send_sem, recv_sem, local_sem, up_buf, down_buf, weight_sem = refs[27:33]
    pad_ref = scratch[0]
    own = pltpu.make_async_copy(x_ref, pad_ref.at[pl.ds(3, 32)], local_sem)
    own.start()
    greet([neighbour(dr, dc) for dr, dc in AROUND])
    copies = start_halo(x_ref, edge_ref, (pad_ref.at[pl.ds(0, 3)], pad_ref.at[pl.ds(35, 3)]) + tuple(sides), send_sem, recv_sem)
    landed = fetch((ins[4].at[0], ins[5].at[0]), (up_buf, down_buf), weight_sem)
    rims = []

    def arrived():
        own.wait()
        for copy in copies:
            copy.wait()
        for n, (dr, dc) in enumerate(AROUND):
            slot = (1 - dr) * 3 + 1 - dc
            slot = slot - 1 if slot > 4 else slot
            rims.append(send(norm_ref.at[pl.ds(0, 64)], rims_ref.at[slot], send_sem.at[8 + n], recv_sem.at[8 + n], neighbour(dr, dc)))

    block_body(False, *ins[:4], up_buf, down_buf, ins[6], arrived, landed, sides, out_ref, line_ref, *scratch)
    for copy in rims:
        copy.wait()


def ocean_first(*args):
    scratch = [pltpu.VMEM(*item) for item in BLOCK_SCRATCH + SIDES] + [pltpu.SemaphoreType.DMA((16,))] * 2 + [pltpu.SemaphoreType.DMA] + WEIGHT_SCRATCH
    return pl.pallas_call(
        first_kernel,
        out_shape=(
            jax.ShapeDtypeStruct((32, 8, 16, 256), BF16), jax.ShapeDtypeStruct((6, 32, 256), BF16),
            jax.ShapeDtypeStruct((8, 64, 512), BF16)),
        in_specs=[vmem()] * 4 + [anywhere()] * 2 + [vmem(), anywhere(), vmem(), vmem()],
        out_specs=(vmem(), vmem(), anywhere()),
        scratch_shapes=scratch,
        compiler_params=pltpu.CompilerParams(vmem_limit_bytes=60 << 20, collective_id=1, has_side_effects=True),
        name="ocean_first",
    )(*args)


def last_kernel(*refs):
    ins, x_ref, north_ref, south_ref, sides = refs[:7], refs[7], refs[8], refs[9], refs[10:16]
    out_ref, scratch, sems = refs[16], refs[17:25], refs[25]
    up_buf, down_buf, weight_sem = refs[26:29]
    pad_ref = scratch[0]
    copies = [
        pltpu.make_async_copy(x_ref, pad_ref.at[pl.ds(3, 32)], sems.at[0]),
        pltpu.make_async_copy(north_ref, pad_ref.at[pl.ds(0, 3)], sems.at[1]),
        pltpu.make_async_copy(south_ref, pad_ref.at[pl.ds(35, 3)], sems.at[2])]
    for copy in copies:
        copy.start()

    def arrived():
        for copy in copies:
            copy.wait()

    landed = fetch((ins[4].at[1], ins[5].at[1]), (up_buf, down_buf), weight_sem)
    block_body(True, *ins[:4], up_buf, down_buf, ins[6], arrived, landed, sides, out_ref, None, *scratch)


def ocean_last(*args):
    return pl.pallas_call(
        last_kernel,
        out_shape=jax.ShapeDtypeStruct((32, 128, 256), BF16),
        in_specs=[vmem()] * 4 + [anywhere()] * 2 + [vmem()] + [anywhere()] * 3 + [vmem()] * 6,
        out_specs=vmem(),
        scratch_shapes=[pltpu.VMEM(*item) for item in BLOCK_SCRATCH] + [pltpu.SemaphoreType.DMA((3,))] + WEIGHT_SCRATCH,
        compiler_params=pltpu.CompilerParams(vmem_limit_bytes=60 << 20),
        name="ocean_last",
    )(*args)


def front_kernel(wflux_ref, fields_ref, cols_ref, fluxw_ref, state_hbm, mask_ref, wfin_ref, scols_ref, sw_ref, state_ref, wsurf_ref,
                 gain_ref, x_ref, edge_ref, atm_ref, norm_ref, flux_own, field_own, flux_tab, field_tab, lines_ref,
                 flux_send, flux_recv, field_send, field_recv, pass_send, pass_recv, ocean_ref, ocean_sem):
    landed = fetch((state_hbm,), (ocean_ref,), ocean_sem)
    me = lax.axis_index("lon")
    side, deep = me // 8, lax.rem(me, 8)
    partner = {"lon": lax.rem(me + 8, 16)}
    high, low = split(wflux_ref[...])
    both = contract_last(jnp.concatenate([high, low], axis=0), state_ref[...])
    fluxes = jnp.concatenate([both[0:4] + both[4:8], jnp.zeros((12, 128), F32)], axis=0).astype(BF16)
    fields = fields_ref[...].astype(BF16)
    flux_own[...] = fluxes
    field_own[...] = fields
    flux_tab[me] = fluxes
    field_tab[me] = fields
    greet([{"lon": lax.rem(me + step, 16)} for step in range(1, 16)])
    small_copies = [
        send(flux_own, flux_tab.at[me], flux_send.at[step], flux_recv.at[step], {"lon": lax.rem(me + step, 16)})
        for step in range(1, 16)]
    field_copies = [
        send(field_own, field_tab.at[me], field_send.at[step], field_recv.at[step], {"lon": side * 8 + lax.rem(deep + step, 8)})
        for step in range(1, 8)]
    pass_copies = [send(field_own, field_tab.at[me], pass_send.at[0], pass_recv.at[0], partner)]
    for copy in small_copies:
        copy.wait()
    landed()

    pairs = []
    for p in range(8):
        pairs.append(jnp.concatenate([flux_tab[2 * p, 0:4], flux_tab[2 * p + 1, 0:4]], axis=0))
    small = jnp.concatenate(pairs, axis=0)
    node = iota((128, 128), 0)
    half = iota((8, 128), 0) // 4
    wide = jnp.concatenate([wfin_ref[...], wfin_ref[...]], axis=0)
    whigh, wlow = split(wide)
    zero8 = jnp.zeros((8, 256), BF16)
    right = jnp.concatenate([
        jnp.concatenate([whigh, zero8], axis=1), jnp.concatenate([whigh, zero8], axis=1),
        jnp.concatenate([wlow, zero8], axis=1), jnp.concatenate([zero8, jnp.ones((8, 256), BF16)], axis=1)], axis=0)
    order = order_matrix().astype(BF16)
    top_row = iota((8, 128), 0) == 0

    def row(r, carry):
        ids = [cols_ref[k, pl.ds(r, 1)] for k in range(4)]
        hots = [jnp.where(node == (i & 127), 1.0, 0.0).astype(BF16) for i in ids]
        picked = jnp.dot(small, jnp.concatenate(hots, axis=1), preferred_element_type=F32)
        cell = None
        for k in range(4):
            part = (ids[k] >> 7) & 15
            level = part >> 1
            total = None
            for p in range(8):
                term = jnp.where(level == p, picked[8 * p : 8 * p + 8, 128 * k : 128 * k + 128], 0.0)
                total = term if total is None else total + term
            total = jnp.where(half == (part & 1), total, 0.0) * fluxw_ref[k, pl.ds(r, 1)]
            cell = total if cell is None else cell + total
        high, low = split(cell)
        sea = jnp.where(top_row, mask_ref[pl.ds(r, 1)].astype(F32), 0.0).astype(BF16)
        both = contract_first(jnp.concatenate([high, low, high, sea], axis=0), right)
        fresh = both[:, 256:512] * (ocean_ref[r].astype(F32) + both[:, 0:256])
        fresh16 = fresh.astype(BF16)
        x_ref[r] = jnp.dot(order, fresh16, preferred_element_type=F32).astype(BF16).reshape(8, 16, 256)
        keep_edges(lines_ref, r, fresh, (0, 1, 2, 125, 126, 127))
        return carry

    lax.fori_loop(0, 16, row, 0, unroll=8)
    for step in range(1, 8):
        field_copies[step - 1].wait()
        block = field_tab.at[side * 8 + lax.rem(deep + 8 - step, 8)]
        pass_copies.append(send(block, block, pass_send.at[step], pass_recv.at[step], partner))
    lax.fori_loop(16, 32, row, 0, unroll=8)
    edge_ref[...] = lines_ref[...].astype(BF16)
    for copy in pass_copies:
        copy.wait()

    ids = jnp.concatenate([scols_ref[k : k + 1] for k in range(4)], axis=1)
    cell = ids & 2047
    level = (ids >> 11) & 31
    spot = iota((128, 512), 0)
    hots, tabs = [], []
    for p in range(16):
        hots.append(jnp.where(spot + 128 * p == cell, 1.0, 0.0).astype(BF16))
        tabs.append(field_tab[p])
    picked = jnp.dot(jnp.concatenate(tabs, axis=1), jnp.concatenate(hots, axis=0), preferred_element_type=F32)
    weight = jnp.concatenate([sw_ref[k : k + 1] for k in range(4)], axis=1)
    chosen = jnp.where(iota((32, 512), 0) == level, weight, 0.0)
    sums = []
    for s in range(4):
        term = jnp.sum(picked[32 * s : 32 * s + 32] * chosen, axis=0, keepdims=True)
        sums.append(term[:, 0:128] + term[:, 128:256] + term[:, 256:384] + term[:, 384:512])
    nodes = jnp.concatenate(sums + [jnp.zeros((4, 128), F32)], axis=0)
    high, low = split(nodes)
    whigh, wlow = split(jnp.concatenate([wsurf_ref[...], jnp.zeros((4, 512), F32)], axis=0))
    zeros = jnp.zeros((8, 128), BF16)
    lift = contract_first(jnp.concatenate([high, low, high, zeros], axis=0), jnp.concatenate([whigh, whigh, wlow, jnp.zeros((8, 512), BF16)], axis=0))
    atm_in = state_ref[...].astype(F32) + lift
    atm_ref[...] = atm_in
    norm_ref[...] = unit_norm(atm_in, gain_ref[...], 1e-5).astype(BF16)


def front(*args):
    return pl.pallas_call(
        front_kernel,
        out_shape=(
            jax.ShapeDtypeStruct((32, 8, 16, 256), BF16),
            jax.ShapeDtypeStruct((6, 32, 256), BF16),
            jax.ShapeDtypeStruct((128, 512), F32),
            jax.ShapeDtypeStruct((128, 512), BF16),
        ),
        in_specs=[vmem()] * 4 + [anywhere()] + [vmem()] * (len(args) - 5),
        out_specs=tuple([vmem()] * 4),
        scratch_shapes=[
            pltpu.VMEM((16, 128), BF16), pltpu.VMEM((128, 128), BF16), pltpu.VMEM((16, 16, 128), BF16), pltpu.VMEM((16, 128, 128), BF16),
            pltpu.VMEM((6, 32, 256), F32)] + [pltpu.SemaphoreType.DMA((16,))] * 2 + [pltpu.SemaphoreType.DMA((8,))] * 4
        + [pltpu.VMEM((32, 128, 256), BF16), pltpu.SemaphoreType.DMA((1,))],
        compiler_params=pltpu.CompilerParams(vmem_limit_bytes=60 << 20, collective_id=0, has_side_effects=True),
        name="front",
    )(*args)


def silu(values):
    return values * jax.nn.sigmoid(values)


def atmosphere_kernel(norm_ref, rims_ref, atm_ref, edges_hbm, near_ref, degree_ref, wq_hbm, wk_hbm, wv_hbm, wo_hbm, win_hbm, wsrc_hbm,
                      wdst_hbm, wout_hbm, wbias_ref, gain_ref, up_hbm, down_hbm, x_ref, line_ref, out_ref, edge_out_ref, *rest):
    greet([neighbour(dr, dc) for dr, dc in AROUND])
    copies = start_halo(x_ref, line_ref, rest[:8], rest[8], rest[9])
    early = (wk_hbm, wv_hbm, wdst_hbm, wq_hbm, wsrc_hbm, edges_hbm, win_hbm, wout_hbm)
    ready = fetch(early, rest[10:18], rest[21])
    ready_late = fetch((wo_hbm, up_hbm, down_hbm), rest[18:21], rest[22])
    wk_ref, wv_ref, wdst_ref, wq_ref, wsrc_ref, edges_ref, win_ref, wout_ref, wo_ref, up_ref, down_ref = rest[10:21]
    band = lax.axis_index("comp") * 8 + lax.axis_index("lat")
    col = lax.axis_index("lon")
    ids = near_ref[...]
    part, inside = ids >> 7, ids & 127
    down = (part >> 4) - band
    right = (((part & 15) - col + 1) & 15) - 1
    spot = (down + 1) * 3 + right + 1
    spot = spot - jnp.where(spot > 4, 1, 0)
    at = jnp.where((down == 0) & (right == 0), inside, 128 + spot * 64 + inside)
    info = jnp.concatenate([at, degree_ref[...], degree_ref[...]], axis=0).astype(F32)
    info = info.T
    table = jnp.concatenate([norm_ref[...], rims_ref[...]], axis=0)
    lane = iota((128, 640), 1).astype(F32)
    hots = [jnp.where(lane == info[:, k : k + 1], 1.0, 0.0).astype(BF16) for k in range(6)]
    near = jnp.dot(jnp.concatenate(hots, axis=0), table, preferred_element_type=F32).astype(BF16)
    ready()
    keys = jnp.dot(near, wk_ref[...], preferred_element_type=F32).astype(BF16)
    values = jnp.dot(near, wv_ref[...], preferred_element_type=F32).astype(BF16)
    far = jnp.dot(near, wdst_ref[...], preferred_element_type=F32).astype(BF16)
    query = jnp.dot(norm_ref[...], wq_ref[...], preferred_element_type=F32).astype(BF16).astype(F32)
    own = jnp.dot(norm_ref[...], wsrc_ref[...], preferred_element_type=F32)
    edges = edges_ref[...].reshape(768, 512)
    before = jnp.dot(edges, win_ref[...], preferred_element_type=F32)
    hidden = []
    for k in range(6):
        rows = slice(128 * k, 128 * k + 128)
        hidden.append(silu(before[rows] + own + far[rows].astype(F32)).astype(BF16))
    edge_sum = edges.astype(F32) + jnp.dot(jnp.concatenate(hidden, axis=0), wout_ref[...], preferred_element_type=F32)
    edge_out_ref[...] = edge_sum.astype(BF16).reshape(6, 128, 512)
    head = jnp.where(iota((8, 512), 0) == iota((8, 512), 1) // 64, 1.0, 0.0)
    scaled = (head * 0.125).astype(BF16)
    bhigh, blow = split(wbias_ref[...])
    mixer = jnp.concatenate([scaled, scaled, bhigh, bhigh, blow], axis=1)
    scores = []
    for k in range(6):
        rows = slice(128 * k, 128 * k + 128)
        qhigh, qlow = split(query * keys[rows].astype(F32))
        ehigh, elow = split(edge_sum[rows])
        score = contract_last(jnp.concatenate([qhigh, qlow, ehigh, elow, ehigh], axis=1), mixer)
        scores.append(jnp.where(info[:, 6:7] > k, score, -1e30))
    most = functools.reduce(jnp.maximum, scores)
    powers = [jnp.exp(score - most) for score in scores]
    total = functools.reduce(jnp.add, powers)
    attended = None
    for k in range(6):
        weight = (powers[k] / total).astype(BF16)
        spread = jnp.dot(weight, head.astype(BF16), preferred_element_type=F32)
        term = spread * values[128 * k : 128 * k + 128].astype(F32)
        attended = term if attended is None else attended + term
    ready_late()
    middle = atm_ref[...] + jnp.dot(attended.astype(BF16), wo_ref[...], preferred_element_type=F32)
    normed2 = unit_norm(middle, gain_ref[...], 1e-5).astype(BF16)
    expanded = silu(jnp.dot(normed2, up_ref[...], preferred_element_type=F32)).astype(BF16)
    out_ref[...] = (middle + jnp.dot(expanded, down_ref[...], preferred_element_type=F32)).astype(BF16)
    for copy in copies:
        copy.wait()


def atmosphere(*args):
    return pl.pallas_call(
        atmosphere_kernel,
        out_shape=(jax.ShapeDtypeStruct((128, 512), BF16), jax.ShapeDtypeStruct((6, 128, 512), BF16))
        + tuple(jax.ShapeDtypeStruct(*item) for item in ROWS + SIDES),
        in_specs=[vmem()] * 3 + [anywhere()] + [vmem()] * 2 + [anywhere()] * 8 + [vmem()] * 2 + [anywhere()] * 4,
        out_specs=(vmem(), vmem()) + (anywhere(),) * 8,
        scratch_shapes=[pltpu.SemaphoreType.DMA((8,))] * 2 + [pltpu.VMEM((512, 512), BF16)] * 5 + [pltpu.VMEM((6, 128, 512), BF16)]
        + [pltpu.VMEM((512, 512), BF16)] * 3 + [pltpu.VMEM((512, 2048), BF16), pltpu.VMEM((2048, 512), BF16)]
        + [pltpu.SemaphoreType.DMA((8,)), pltpu.SemaphoreType.DMA((3,))],
        compiler_params=pltpu.CompilerParams(vmem_limit_bytes=60 << 20, collective_id=2, has_side_effects=True),
        name="atmosphere",
    )(*args)


def local(atm_state, edge_state, neighbours, degree, surface_fields, ocean_state, wet_mask, flux_columns, flux_weights,
          surface_columns, surface_weights, w_surface, w_flux, ln1_gain, w_query, w_key, w_value, w_out, w_edge_in, w_edge_src,
          w_edge_dst, w_edge_out, w_bias, ln2_gain, w_up, w_down, w_flux_in, dw_kernel, dw_bias, ocean_gain, w_expand, w_reduce,
          layer_scale):
    x, edge, atm_in, normed = front(
        w_flux.T, surface_fields.reshape(128, 128), flux_columns, flux_weights, ocean_state, wet_mask, w_flux_in, surface_columns,
        surface_weights, atm_state, w_surface, ln1_gain.reshape(1, 512))
    ocean = (dw_kernel.transpose(1, 0, 2), dw_bias, ocean_gain, layer_scale, w_expand, w_reduce, wet_mask)
    x, edge, rims = ocean_first(*ocean, x, edge, normed)
    atm_out, edge_out, *halo = atmosphere(
        normed, rims.reshape(512, 512), atm_in, edge_state.transpose(1, 0, 2), neighbours.T, degree.reshape(1, 128), w_query, w_key,
        w_value, w_out, w_edge_in, w_edge_src, w_edge_dst, w_edge_out, w_bias.T, ln2_gain.reshape(1, 512), w_up, w_down, x, edge)
    ocean_out = ocean_last(*ocean, x, *halo)
    return atm_out, edge_out.transpose(1, 0, 2), ocean_out


def solution(mesh):
    whole, rows = ("comp", "lat", "lon"), ("comp", "lat")
    in_specs = (
        P(whole, None), P(whole, None, None), P(whole, None), P(whole), P(None, rows, "lon"), P(rows, "lon", None), P(rows, "lon"),
        P(None, rows, "lon"), P(None, rows, "lon"), P(None, whole), P(None, whole)) + (P(),) * 22
    out_specs = (P(whole, None), P(whole, None, None), P(rows, "lon", None))
    return jax.shard_map(local, mesh=mesh, in_specs=in_specs, out_specs=out_specs, check_vma=False)
```
